256 devices in a mesh: learn: 8 (over x, y_hi), act: 32 (over y_lo, z, core).
Axes of the slice: x: 4, y: 4 (y_hi: 2, y_lo: 2; y = y_hi * 2 + y_lo), z: 8, core: 2. Of those that a mesh axis runs over, the one named last changes fastest.
Arguments:
- positions: int32 [2, 256, 361], P(None, ('learn', 'act')), may hold values from 0 to 2
- to_move: int32 [2, 256], P(None, ('learn', 'act')), may hold values from 0 to 1
- legal_moves: int32 [2, 256, 361], P(None, ('learn', 'act')), may hold values 0 or 1
- master: float32 [8, 2, 2304, 256], P('learn', None, 'act'), may hold values from -0.125 to 0.125
- gradients: float32 [8, 8, 2, 2304, 256], P('learn', None, None, 'act'), may hold values from -0.4375 to 0.4375
- stem_weight: bfloat16 [36, 256], replicated, may hold values from -1 to 1
- policy_weight: float32 [256], replicated, may hold values from -2 to 2
- pass_weight: float32 [256], replicated, may hold values from -2 to 2
- value_weight: float32 [256], replicated, may hold values from -0.375 to 0.375
Outputs:
- updated: float32 [8, 2, 2304, 256], P('learn', None, 'act')
- policy_logp: float32 [2, 256, 362], P(None, ('learn', 'act'))
- value: float32 [2, 256], P(None, ('learn', 'act'))
The draws below stay inside these ranges and needn't reach their ends.
All inputs are finite; a program needn't handle non-finite values. No bound on the sum of `legal_moves` on one device may be relied on, other than what follows from the above.
Results may differ from the reference program's by a relative error of at most 0.008.
Values may be sent and summed in bfloat16 or wider, within the bound.
A program may use at most 128 MiB of HBM per device.

```python
import jax
import jax.numpy as jnp
from jax import lax

C = 256
BOARD = 19
CELLS = 361
PLANES = 4
STEPS = 2
LAYERS = 8
POSITIONS = 256
N_LEARN = 8


def touch_ends(drawn, own_key, smallest, high):
    longest = drawn.shape.index(max(drawn.shape))
    spots = []
    for shift in (0, 1):
        where = [jax.random.randint(jax.random.fold_in(own_key, axis), (), 0, length) for axis, length in enumerate(drawn.shape)]
        where[longest] = (where[longest] + shift) % drawn.shape[longest]
        spots.append(tuple(where))
    return drawn.at[spots[0]].set(smallest).at[spots[1]].set(high)


def with_spikes(entries, stream_key, source, target, parts, factor):
    def block_of(axis_at):
        return (jnp.arange(entries.shape[axis_at]) // (entries.shape[axis_at] // parts)).reshape((-1,) + (1,) * (entries.ndim - 1 - axis_at))

    near = jax.random.permutation(stream_key, parts)[block_of(target)]
    far = (block_of(target) + parts // 2) % parts
    return jnp.where((block_of(source) == near) | (block_of(source) == far), factor * entries, entries)


def level_of(stream_key, extent, cuts, low, top_value):
    level, own = 1.0, jax.random.fold_in(stream_key, 6)
    for position, parts in cuts:
        steps = jnp.exp(jax.random.uniform(jax.random.fold_in(own, position), (parts,), jnp.float32, low / len(cuts), top_value / len(cuts)))
        level = level * jnp.repeat(steps, extent[position] // parts).reshape([-1 if axis == position else 1 for axis in range(len(extent))])
    return level


def noise(key, extent, width, reach, pieces=(), kind=jnp.bfloat16):
    drawn = jax.random.normal(key, extent, jnp.float32) * width
    if len(pieces) > 0:
        drawn = level_of(key, extent, pieces, -0.22, 0.18) * drawn
    return jnp.clip(drawn, min=-reach, max=reach).astype(kind)


def heavy_noise(rng, shape, spread, limit, pieces, heavy, kind=jnp.bfloat16):
    entries = spread * jax.random.normal(rng, shape, jnp.float32)
    if pieces:
        entries = entries * level_of(rng, shape, pieces, -0.22, 0.18)
    return jnp.clip(with_spikes(entries, jax.random.fold_in(rng, 3), *heavy), -limit, limit).astype(kind)


def setup_inputs(seed: int = 0) -> dict:
    keys = jax.random.split(jax.random.key(seed), 10)
    positions = touch_ends(jax.random.randint(keys[0], (STEPS, POSITIONS, CELLS), 0, 3), jax.random.fold_in(keys[0], 1), 0, 2).astype(jnp.int32)
    to_move = touch_ends(jax.random.randint(keys[1], (STEPS, POSITIONS), 0, 2), jax.random.fold_in(keys[1], 1), 0, 1).astype(jnp.int32)
    legal_moves = touch_ends((jax.random.randint(keys[2], (STEPS, POSITIONS, CELLS), 0, 2) < 1).astype(jnp.int32), jax.random.fold_in(keys[2], 1), 0, 1)
    master = noise(keys[3], (LAYERS, 2, 9 * C, C), (9 * C) ** -0.5, 0.125, ((0, 8), (2, 32)), jnp.float32)
    gradients = heavy_noise(keys[4], (N_LEARN, LAYERS, 2, 9 * C, C), (1.0 / (9 * C) ** 0.5), 0.4375, ((0, 8), (3, 32)), (0, 1, 8, 2.0), jnp.float32)
    stem_weight = noise(keys[5], (9 * PLANES, C), (9 * PLANES) ** -0.5, 1.0)
    policy_weight = noise(keys[6], (C,), (2.0 / C ** 0.5), 2.0, (), jnp.float32)
    pass_weight = noise(keys[7], (C,), (2.0 / C ** 0.5), 2.0, (), jnp.float32)
    value_weight = noise(keys[8], (C,), C ** -0.5, 0.375, (), jnp.float32)
    return {"positions": positions, "to_move": to_move, "legal_moves": legal_moves, "master": master, "gradients": gradients, "stem_weight": stem_weight, "policy_weight": policy_weight, "pass_weight": pass_weight, "value_weight": value_weight}


def convolve(planes_in, kernel):
    padded = jnp.pad(planes_in, ((0, 0), (1, 1), (1, 1), (0, 0)))
    shifted = [padded[:, row_off:row_off + BOARD, col_off:col_off + BOARD, :] for row_off in range(3) for col_off in range(3)]
    stacked = jnp.concatenate(shifted, axis=-1)
    unrolled = stacked.reshape(-1, stacked.shape[-1])
    result = jnp.dot(unrolled, kernel, preferred_element_type=jnp.float32)
    return result.reshape(planes_in.shape[0], BOARD, BOARD, kernel.shape[1])


def make_planes(boards, sides):
    side_move = sides[:, None]
    own_stones = boards == 1 + side_move
    foe_stones = boards == 2 - side_move
    vacant = boards == 0
    filled = jnp.ones_like(own_stones)
    stacked = jnp.stack([own_stones, foe_stones, vacant, filled], axis=-1).astype(jnp.bfloat16)
    return stacked.reshape(boards.shape[0], BOARD, BOARD, PLANES)


def heads(stream, legal_rows, policy_weight, pass_weight, value_weight):
    number = stream.shape[0]
    trunk_out = jax.nn.relu(stream).reshape(number, CELLS, stream.shape[-1])
    board_raw = jnp.einsum("pcd,d->pc", trunk_out, policy_weight, precision=lax.Precision.HIGHEST)
    pooled = jnp.mean(trunk_out, axis=1)
    pass_raw = jnp.dot(pooled, pass_weight, precision=lax.Precision.HIGHEST)
    value_raw = jnp.dot(pooled, value_weight, precision=lax.Precision.HIGHEST)
    logits = 10.0 * jnp.tanh(jnp.concatenate([board_raw, pass_raw[:, None]], axis=1) / 10.0)
    allowed = jnp.concatenate([legal_rows, jnp.ones((number, 1), jnp.int32)], axis=1) > 0
    exponent = jnp.where(allowed, jnp.exp(logits), 0.0)
    denominator = jnp.sum(exponent, axis=1, keepdims=True)
    logp = jnp.where(allowed, logits - jnp.log(denominator), 0.0)
    return logp, jnp.tanh(value_raw)


def reference(positions, to_move, legal_moves, master, gradients, stem_weight, policy_weight, pass_weight, value_weight):
    gradient_sum = jnp.sum(gradients, axis=0)
    updated = master - gradient_sum / N_LEARN
    weights = updated.astype(jnp.bfloat16)
    boards = positions.reshape(-1, CELLS)
    sides = to_move.reshape(-1)
    legal_flat = legal_moves.reshape(-1, CELLS)

    def single(items):
        board_one, side_one, legal_one = items
        planes = make_planes(board_one[None], side_one[None])
        stream = convolve(planes, stem_weight)
        for layer in range(LAYERS):
            activ = jax.nn.relu(stream).astype(jnp.bfloat16)
            middle = jax.nn.relu(convolve(activ, weights[layer, 0])).astype(jnp.bfloat16)
            stream = stream + convolve(middle, weights[layer, 1])
        logp, value_one = heads(stream, legal_one[None], policy_weight, pass_weight, value_weight)
        return logp[0], value_one[0]

    logp_all, value_all = lax.map(single, (boards, sides, legal_flat))
    return updated, logp_all.reshape(STEPS, POSITIONS, CELLS + 1), value_all.reshape(STEPS, POSITIONS)
```

```python
import jax
import jax.numpy as jnp
from jax import lax
from jax.experimental import pallas as pl
from jax.experimental.pallas import tpu as pltpu
from jax.sharding import PartitionSpec as P

ROWS = 760
PADR = 840
W2 = 40

def to_rows(x):
    return jnp.pad(x.reshape(2, 19, 19).transpose(1, 0, 2), ((0, 0), (0, 0), (0, 1))).reshape(ROWS)

def net_kernel(code_ref, legal_ref, w_ref, stem_ref, pol_ref, pas_ref, val_ref, logp_ref, head_ref, big, stream, stem_pad):
    col = lax.broadcasted_iota(jnp.int32, (ROWS, 1), 0)
    valid = lax.rem(col, 20) != 19

    def put(a):
        a = jnp.where(valid, jnp.maximum(a, 0.0), 0.0)
        big[W2:W2 + ROWS, 256:512] = a.astype(jnp.bfloat16)
        big[W2:W2 + ROWS, 0:256] = pltpu.roll(a, 1, 0).astype(jnp.bfloat16)
        big[W2:W2 + ROWS, 512:768] = pltpu.roll(a, ROWS - 1, 0).astype(jnp.bfloat16)

    def conv(layer, which):
        acc = jnp.dot(big[0:ROWS, :], w_ref[layer, which, 0:768, :], preferred_element_type=jnp.float32)
        acc += jnp.dot(big[W2:W2 + ROWS, :], w_ref[layer, which, 768:1536, :], preferred_element_type=jnp.float32)
        acc += jnp.dot(big[2 * W2:2 * W2 + ROWS, :], w_ref[layer, which, 1536:2304, :], preferred_element_type=jnp.float32)
        return acc

    big[0:W2, :] = jnp.zeros((W2, 768), jnp.bfloat16)
    big[W2 + ROWS:, :] = jnp.zeros((W2, 768), jnp.bfloat16)
    stem_pad[...] = jnp.zeros_like(stem_pad)
    stem_pad[0:36, :] = stem_ref[...]

    lane = lax.broadcasted_iota(jnp.int32, (ROWS, 128), 1)
    seen = jnp.zeros((ROWS, 128), jnp.float32)
    for b in range(3):
        turned = code_ref[...] if b == 1 else pltpu.roll(code_ref[...], 1 if b == 0 else PADR - 1, 0)
        for a in range(3):
            seen = jnp.where(lane // 4 == 3 * a + b, turned[W2 * a:W2 * a + ROWS, :], seen)
    plane = lane % 4
    feat = jnp.where(plane == 3, jnp.where(seen > 0.0, 1.0, 0.0), jnp.where(seen == (plane + 1).astype(jnp.float32), 1.0, 0.0)).astype(jnp.bfloat16)
    first = jnp.dot(feat, stem_pad[...], preferred_element_type=jnp.float32)
    stream[...] = first
    put(first)

    @pl.loop(0, 8)
    def _(layer):
        put(conv(layer, 0))
        out = stream[...] + conv(layer, 1)
        stream[...] = out
        put(out)

    trunk = jnp.maximum(stream[...], 0.0)
    raw = lax.dot_general(jnp.broadcast_to(pol_ref[...], (8, 256)), trunk, (((1,), (1,)), ((), ())),
                          precision=lax.Precision.HIGHEST, preferred_element_type=jnp.float32)[0:1]
    logits = 10.0 * jnp.tanh(raw / 10.0)
    legal = legal_ref[...] > 0
    expd = jnp.where(legal, jnp.exp(logits), 0.0)
    spot = lax.broadcasted_iota(jnp.int32, (1, ROWS), 1)
    mine = lax.rem(spot // 20, 2)
    mine_col = lax.rem(col // 20, 2)
    lines = jnp.zeros((1, ROWS), jnp.float32)
    small = lax.broadcasted_iota(jnp.int32, (8, 128), 1)
    head = jnp.zeros((8, 128), jnp.float32)
    for q in range(2):
        pooled = jnp.sum(jnp.where(valid & (mine_col == q), trunk, 0.0), axis=0, keepdims=True) / 361.0
        pass_raw = jnp.sum(pooled * pas_ref[...], axis=1, keepdims=True)
        value_raw = jnp.sum(pooled * val_ref[...], axis=1, keepdims=True)
        pass_logit = 10.0 * jnp.tanh(pass_raw / 10.0)
        total = jnp.sum(jnp.where(mine == q, expd, 0.0), axis=1, keepdims=True) + jnp.exp(pass_logit)
        logden = jnp.log(total)
        lines = jnp.where(mine == q, logden, lines)
        head = jnp.where(small == q, pass_logit - logden, head)
        head = jnp.where(small == 2 + q, jnp.tanh(value_raw), head)
    logp_ref[...] = jnp.where(legal, logits - lines, 0.0)
    head_ref[...] = head

def network(positions, to_move, legal_moves, weights, stem, pol, pas, val):
    boards = positions.reshape(2, 361)
    side = to_move.reshape(2, 1)
    code = jnp.where(boards == 1 + side, 1.0, 0.0) + jnp.where(boards == 2 - side, 2.0, 0.0) + jnp.where(boards == 0, 3.0, 0.0)
    code = jnp.broadcast_to(jnp.pad(to_rows(code), (W2, W2))[:, None], (PADR, 128))
    legal = to_rows(legal_moves.reshape(2, 361)).reshape(1, ROWS)
    logp, head = pl.pallas_call(
        net_kernel,
        out_shape=(jax.ShapeDtypeStruct((1, ROWS), jnp.float32), jax.ShapeDtypeStruct((8, 128), jnp.float32)),
        in_specs=[pl.BlockSpec(memory_space=pltpu.VMEM)] * 7,
        out_specs=(pl.BlockSpec(memory_space=pltpu.VMEM),) * 2,
        scratch_shapes=[pltpu.VMEM((PADR, 768), jnp.bfloat16), pltpu.VMEM((ROWS, 256), jnp.float32), pltpu.VMEM((128, 256), jnp.bfloat16)],
        compiler_params=pltpu.CompilerParams(vmem_limit_bytes=56 << 20),
    )(code, legal, weights, stem, pol.reshape(1, 256), pas.reshape(1, 256), val.reshape(1, 256))
    board = logp.reshape(19, 2, 20)[:, :, :19].transpose(1, 0, 2).reshape(2, 361)
    full = jnp.concatenate([board, head[0, 0:2].reshape(2, 1)], axis=1).reshape(2, 1, 362)
    return full, head[0, 2:4].reshape(2, 1)


def per_device(positions, to_move, legal_moves, master, gradients, stem_weight, policy_weight, pass_weight, value_weight):
    gradient_sum = lax.psum_scatter(gradients[0], "learn", scatter_dimension=0, tiled=True)
    updated = master - gradient_sum / 8
    sending = updated.astype(jnp.bfloat16)
    stacked = lax.all_gather(sending, "learn", axis=0, tiled=True)
    complete = lax.all_gather(stacked, "act", axis=2, tiled=True)
    logp, value = network(positions, to_move, legal_moves, complete, stem_weight, policy_weight, pass_weight, value_weight)
    return updated, logp, value


def solution(mesh):
    spread = P(None, ("learn", "act"), None)
    in_specs = (spread, P(None, ("learn", "act")), spread, P("learn", None, "act", None),
                P("learn", None, None, "act", None), P(), P(), P(), P())
    out_specs = (P("learn", None, "act", None), spread, P(None, ("learn", "act")))
    return jax.shard_map(per_device, mesh=mesh, in_specs=in_specs, out_specs=out_specs, check_vma=False)
```

```python
import jax
import jax.numpy as jnp
from jax import lax
from jax.experimental import pallas as pl
from jax.experimental.pallas import tpu as pltpu
from jax.sharding import PartitionSpec as P

MESH = pl.DeviceIdType.MESH
ROWS = 760
PADR = 840
W2 = 40
SPLIT = 40
CHUNKS = 8
LAG = 5


def to_rows(x):
    return jnp.pad(x.reshape(2, 19, 19).transpose(1, 0, 2), ((0, 0), (0, 0), (0, 1))).reshape(ROWS)


def device(x, y, z, c):
    y = lax.rem(y + 4, 4)
    return (lax.rem(x + 4, 4) * 2 + y // 2, (lax.rem(y, 2) * 8 + lax.rem(z + 8, 8)) * 2 + c)


def body(code_ref, legal_ref, master_ref, grad_ref, stem_ref, pol_ref, pas_ref, val_ref,
         updated_ref, logp_ref, head_ref,
         w, slots, staged, own, packed, big, stream, stem_pad, s_grad, r_grad, s_own, r_own, l_sem, s_sem, r_sem):
    learn, act = lax.axis_index("learn"), lax.axis_index("act")
    x, y_hi = learn // 2, lax.rem(learn, 2)
    c, z, y_lo = lax.rem(act, 2), lax.rem(act // 2, 8), act // 16
    y = y_hi * 2 + y_lo
    zh, zl = z // 4, lax.rem(z, 4)
    sibling = device(x, y, z, 1 - c)
    learners = [(lax.rem(learn + d, 8), act) for d in range(1, 8)]
    along_z = [device(x, y, z + d, c) for d in range(1, 8)]
    along_x = [device(x + d, y, z, c) for d in range(1, 4)]
    x_up, x_down = device(x + 1, y, z, c), device(x - 1, y, z, c)
    y_up, y_down = device(x, y + 1, z, c), device(x, y - 1, z, c)
    xu, xd = lax.rem(x + 1, 4), lax.rem(x + 3, 4)
    yu, yd = lax.rem(y + 1, 4), lax.rem(y + 3, 4)
    x_rows, y_rows = pl.ds(0, SPLIT), pl.ds(SPLIT, 72 - SPLIT)

    barrier = pltpu.get_barrier_semaphore()
    peers = learners + along_z + [y_up, y_down, sibling]
    for peer in peers:
        pl.semaphore_signal(barrier, inc=1, device_id=peer, device_id_type=MESH)

    take = pltpu.make_async_copy(grad_ref.at[learn], own, l_sem)
    take.start()
    pl.semaphore_wait(barrier, len(peers))

    def send(src, dst, s, r, to):
        copy = pltpu.make_async_remote_copy(src_ref=src, dst_ref=dst, send_sem=s, recv_sem=r, device_id=to, device_id_type=MESH)
        copy.start()

    def arrived(ref, sem):
        pltpu.make_async_copy(ref, ref, sem).wait()

    for d in range(1, 8):
        send(grad_ref.at[lax.rem(learn + d, 8)], slots.at[d - 1], s_grad, r_grad, learners[d - 1])

    col = lax.broadcasted_iota(jnp.int32, (ROWS, 1), 0)
    valid = lax.rem(col, 20) != 19

    def put(a):
        a = jnp.where(valid, jnp.maximum(a, 0.0), 0.0)
        big[W2:W2 + ROWS, 256:512] = a.astype(jnp.bfloat16)
        big[W2:W2 + ROWS, 0:256] = pltpu.roll(a, 1, 0).astype(jnp.bfloat16)
        big[W2:W2 + ROWS, 512:768] = pltpu.roll(a, ROWS - 1, 0).astype(jnp.bfloat16)

    def conv(layer, which):
        for b in range(16):
            halves = [w[layer, which, b // 8, (b // 4) % 2, b % 4, i].astype(jnp.float32) for i in range(2)]
            packed[144 * b:144 * b + 144, :] = jnp.concatenate(halves, axis=0).astype(jnp.bfloat16)
        acc = jnp.dot(big[0:ROWS, :], packed[0:768, :], preferred_element_type=jnp.float32)
        acc += jnp.dot(big[W2:W2 + ROWS, :], packed[768:1536, :], preferred_element_type=jnp.float32)
        acc += jnp.dot(big[2 * W2:2 * W2 + ROWS, :], packed[1536:2304, :], preferred_element_type=jnp.float32)
        return acc

    big[0:W2, :] = jnp.zeros((W2, 768), jnp.bfloat16)
    big[W2 + ROWS:, :] = jnp.zeros((W2, 768), jnp.bfloat16)
    stem_pad[...] = jnp.zeros_like(stem_pad)
    stem_pad[0:36, :] = stem_ref[...]
    lane = lax.broadcasted_iota(jnp.int32, (ROWS, 128), 1)
    seen = jnp.zeros((ROWS, 128), jnp.float32)
    for b in range(3):
        turned = code_ref[...] if b == 1 else pltpu.roll(code_ref[...], 1 if b == 0 else PADR - 1, 0)
        for a in range(3):
            seen = jnp.where(lane // 4 == 3 * a + b, turned[W2 * a:W2 * a + ROWS, :], seen)
    plane = lane % 4
    feat = jnp.where(plane == 3, jnp.where(seen > 0.0, 1.0, 0.0), jnp.where(seen == (plane + 1).astype(jnp.float32), 1.0, 0.0)).astype(jnp.bfloat16)
    first = jnp.dot(feat, stem_pad[...], preferred_element_type=jnp.float32)
    stream[...] = first
    put(first)

    take.wait()
    arrived(slots, r_grad)
    total = own[...]
    for d in range(7):
        total = total + slots[d]
    fresh = master_ref[...] - total / 8
    updated_ref[...] = fresh
    staged[x] = fresh.astype(jnp.bfloat16)
    for to in along_x:
        send(staged.at[x], staged.at[x], s_own, r_own, to)
    arrived(staged.at[pl.ds(0, 3)], r_own)
    for p in range(4):
        for h in range(2):
            w[2 * p + y_hi, h, y_lo, zh, zl, c, y_rows, :] = staged[p, h, SPLIT:, :]

    @pl.when(zl == x)
    def _():
        for p in range(4):
            for h in range(2):
                w[2 * p + y_hi, h, y_lo, zh, zl, c, x_rows, :] = staged[p, h, 0:SPLIT, :]

    def send_z(k):
        layer, h = (k // 2) * 2 + y_hi, lax.rem(k, 2)
        part = w.at[layer, h, y_lo, zh, zl, c, y_rows]
        whole = w.at[layer, h, y_lo, zh, zl, c, x_rows]

        @pl.when(zl == x)
        def _():
            for to in along_z:
                send(whole, whole, s_sem.at[1], r_sem.at[1, k], to)
        for to in along_z:
            send(part, part, s_sem.at[0], r_sem.at[0, k], to)

    def wait_z(k):
        arrived(w.at[pl.ds(0, 7), 0, 0, 0, 0, c, y_rows], r_sem.at[0, k])

        @pl.when(zl == x)
        def _():
            arrived(w.at[pl.ds(0, 1), 0, 0, 0, 0, c, x_rows], r_sem.at[1, k])

        @pl.when(zl != x)
        def _():
            arrived(w.at[pl.ds(0, 2), 0, 0, 0, 0, c, x_rows], r_sem.at[1, k])

    def send_y1(k):
        layer, h = (k // 2) * 2 + y_hi, lax.rem(k, 2)
        part = w.at[layer, h, y_lo, :, :, c, y_rows]
        whole = w.at[layer, h, y_lo, :, x, c, x_rows]
        for to in (y_up, y_down):
            send(whole, whole, s_sem.at[3], r_sem.at[3, k], to)
            send(part, part, s_sem.at[2], r_sem.at[2, k], to)

    def wait_y1(k):
        arrived(w.at[pl.ds(0, 2), 0, 0, :, :, c, y_rows], r_sem.at[2, k])
        arrived(w.at[pl.ds(0, 2), 0, 0, :, 0, c, x_rows], r_sem.at[3, k])

    def send_y2(k):
        for side, half, to in ((yd, 0, y_up), (yu, 1, y_down)):
            layer, h, lo = (k // 2) * 2 + side // 2, lax.rem(k, 2), lax.rem(side, 2)
            part = w.at[layer, h, lo, half, :, c, y_rows]
            whole = w.at[layer, h, lo, half, x, c, x_rows]
            send(whole, whole, s_sem.at[5], r_sem.at[5, k], to)
            send(part, part, s_sem.at[4], r_sem.at[4, k], to)

    def wait_y2(k):
        arrived(w.at[pl.ds(0, 2), 0, 0, 0, :, c, y_rows], r_sem.at[4, k])
        arrived(w.at[pl.ds(0, 2), 0, 0, 0, 0, c, x_rows], r_sem.at[5, k])

    def send_x1(k):
        layer, h = (k // 2) * 2, lax.rem(k, 2)
        part = w.at[pl.ds(layer, 2), h, :, :, x, c, x_rows]
        for to in (x_up, x_down):
            send(part, part, s_sem.at[6], r_sem.at[6, k], to)

    def wait_x1(k):
        arrived(w.at[pl.ds(0, 4), 0, :, :, 0, c, x_rows], r_sem.at[6, k])

    def send_x2(k):
        layer, h = (k // 2) * 2, lax.rem(k, 2)
        for side, half, to in ((xd, 0, x_up), (xu, 1, x_down)):
            part = w.at[layer + half, h, :, :, side, c, x_rows]
            send(part, part, s_sem.at[7], r_sem.at[7, k], to)

    def wait_x2(k):
        arrived(w.at[pl.ds(0, 2), 0, :, :, 0, c, x_rows], r_sem.at[7, k])

    def send_s(k):
        layer, h = (k // 2) * 2, lax.rem(k, 2)
        part = w.at[pl.ds(layer, 2), h, :, :, :, c]
        send(part, part, s_sem.at[8], r_sem.at[8, k], sibling)

    def wait_s(k):
        arrived(w.at[pl.ds(0, 2), 0, :, :, :, c], r_sem.at[8, k])

    send_z(0)
    send_z(1)

    def turn(t, carry):
        @pl.when(t < CHUNKS)
        def _():
            wait_z(t)
            send_y1(t)

        @pl.when(t + 2 < CHUNKS)
        def _():
            send_z(t + 2)

        @pl.when((t >= 1) & (t - 1 < CHUNKS))
        def _():
            wait_y1(t - 1)
            send_y2(t - 1)

        @pl.when((t >= 2) & (t - 2 < CHUNKS))
        def _():
            wait_y2(t - 2)
            send_x1(t - 2)

        @pl.when((t >= 3) & (t - 3 < CHUNKS))
        def _():
            wait_x1(t - 3)
            send_x2(t - 3)

        @pl.when((t >= 4) & (t - 4 < CHUNKS))
        def _():
            wait_x2(t - 4)
            send_s(t - 4)

        @pl.when(t >= LAG)
        def _():
            k = t - LAG
            wait_s(k)

            @pl.when(k >= 1)
            def _():
                out = stream[...] + conv(k - 1, 1)
                stream[...] = out
                put(out)
            put(conv(k, 0))
        return carry

    lax.fori_loop(0, CHUNKS + LAG, turn, 0)
    stream[...] = stream[...] + conv(7, 1)

    trunk = jnp.maximum(stream[...], 0.0)
    raw = lax.dot_general(jnp.broadcast_to(pol_ref[...], (8, 256)), trunk, (((1,), (1,)), ((), ())),
                          precision=lax.Precision.HIGHEST, preferred_element_type=jnp.float32)[0:1]
    logits = 10.0 * jnp.tanh(raw / 10.0)
    legal = legal_ref[...] > 0
    expd = jnp.where(legal, jnp.exp(logits), 0.0)
    spot = lax.broadcasted_iota(jnp.int32, (1, ROWS), 1)
    mine = lax.rem(spot // 20, 2)
    mine_col = lax.rem(col // 20, 2)
    lines = jnp.zeros((1, ROWS), jnp.float32)
    small = lax.broadcasted_iota(jnp.int32, (8, 128), 1)
    head = jnp.zeros((8, 128), jnp.float32)
    for q in range(2):
        pooled = jnp.sum(jnp.where(valid & (mine_col == q), trunk, 0.0), axis=0, keepdims=True) / 361.0
        pass_raw = jnp.sum(pooled * pas_ref[...], axis=1, keepdims=True)
        value_raw = jnp.sum(pooled * val_ref[...], axis=1, keepdims=True)
        pass_logit = 10.0 * jnp.tanh(pass_raw / 10.0)
        total = jnp.sum(jnp.where(mine == q, expd, 0.0), axis=1, keepdims=True) + jnp.exp(pass_logit)
        logden = jnp.log(total)
        lines = jnp.where(mine == q, logden, lines)
        head = jnp.where(small == q, pass_logit - logden, head)
        head = jnp.where(small == 2 + q, jnp.tanh(value_raw), head)
    logp_ref[...] = jnp.where(legal, logits - lines, 0.0)
    head_ref[...] = head

    arrived(slots, s_grad)
    arrived(staged.at[pl.ds(0, 3)], s_own)
    arrived(w.at[pl.ds(0, 7), :, 0, 0, :, c, y_rows], s_sem.at[0])

    @pl.when(zl == x)
    def _():
        arrived(w.at[pl.ds(0, 7), :, 0, 0, :, c, x_rows], s_sem.at[1])
    arrived(w.at[:, 0, :, :, :, c, y_rows], s_sem.at[2])
    arrived(w.at[:, 0, :, :, 0, c, x_rows], s_sem.at[3])
    arrived(w.at[:, 0, 0, :, :, c, y_rows], s_sem.at[4])
    arrived(w.at[:, 0, 0, :, 0, c, x_rows], s_sem.at[5])
    arrived(w.at[:, 0, :, :, :, c, x_rows], s_sem.at[6])
    arrived(w.at[:, 0, :, :, pl.ds(0, 2), c, x_rows], s_sem.at[7])
    arrived(w.at[:, :, :, :, :, c], s_sem.at[8])


def per_device(positions, to_move, legal_moves, master, gradients, stem, pol, pas, val):
    boards = positions.reshape(2, 361)
    side = to_move.reshape(2, 1)
    code = jnp.where(boards == 1 + side, 1.0, 0.0) + jnp.where(boards == 2 - side, 2.0, 0.0) + jnp.where(boards == 0, 3.0, 0.0)
    code = jnp.broadcast_to(jnp.pad(to_rows(code), (W2, W2))[:, None], (PADR, 128))
    legal = to_rows(legal_moves.reshape(2, 361)).reshape(1, ROWS)
    vmem = pl.BlockSpec(memory_space=pltpu.VMEM)
    f32, bf16, dma = jnp.float32, jnp.bfloat16, pltpu.SemaphoreType.DMA
    updated, logp, head = pl.pallas_call(
        body,
        out_shape=(jax.ShapeDtypeStruct((2, 72, 256), f32), jax.ShapeDtypeStruct((1, ROWS), f32), jax.ShapeDtypeStruct((8, 128), f32)),
        in_specs=[vmem, vmem, vmem, pl.BlockSpec(memory_space=pl.ANY), vmem, vmem, vmem, vmem],
        out_specs=(vmem, vmem, vmem),
        scratch_shapes=[
            pltpu.VMEM((8, 2, 2, 2, 4, 2, 72, 256), bf16),
            pltpu.VMEM((7, 2, 72, 256), f32),
            pltpu.VMEM((4, 2, 72, 256), bf16),
            pltpu.VMEM((2, 72, 256), f32),
            pltpu.VMEM((2304, 256), bf16),
            pltpu.VMEM((PADR, 768), bf16),
            pltpu.VMEM((ROWS, 256), f32),
            pltpu.VMEM((128, 256), bf16),
            dma, dma, dma, dma, dma, dma((9,)), dma((9, CHUNKS)),
        ],
        compiler_params=pltpu.CompilerParams(collective_id=0, has_side_effects=True, vmem_limit_bytes=56 << 20),
    )(code, legal, master.reshape(2, 72, 256), gradients.reshape(8, 2, 72, 256), stem,
      pol.reshape(1, 256), pas.reshape(1, 256), val.reshape(1, 256))
    board = logp.reshape(19, 2, 20)[:, :, :19].transpose(1, 0, 2).reshape(2, 361)
    full = jnp.concatenate([board, head[0, 0:2].reshape(2, 1)], axis=1).reshape(2, 1, 362)
    return updated.reshape(1, 2, 72, 256), full, head[0, 2:4].reshape(2, 1)


def solution(mesh):
    spread = P(None, ("learn", "act"), None)
    in_specs = (spread, P(None, ("learn", "act")), spread, P("learn", None, "act", None),
                P("learn", None, None, "act", None), P(), P(), P(), P())
    out_specs = (P("learn", None, "act", None), spread, P(None, ("learn", "act")))
    return jax.shard_map(per_device, mesh=mesh, in_specs=in_specs, out_specs=out_specs, check_vma=False)
```

```python
import jax
import jax.numpy as jnp
from jax import lax
from jax.experimental import pallas as pl
from jax.experimental.pallas import tpu as pltpu
from jax.sharding import PartitionSpec as P

MESH = pl.DeviceIdType.MESH
ROWS = 760
PADR = 840
W2 = 40
SPLIT = 40
CHUNKS = 8
LAG = 3


def device(x, y, z, c):
    y = lax.rem(y + 4, 4)
    return (lax.rem(x + 4, 4) * 2 + y // 2, (lax.rem(y, 2) * 8 + lax.rem(z + 8, 8)) * 2 + c)


def body(pos_ref, side_ref, legal_ref, master_ref, grad_ref, stem_ref, pol_ref, pas_ref, val_ref,
         updated_ref, logp_ref, value_ref,
         w, slots, staged, own, packed, big, stream, stem_pad, spots, s_grad, r_grad, s_own, r_own, l_sem, s_sem, r_sem):
    learn, act = lax.axis_index("learn"), lax.axis_index("act")
    x, y_hi = learn // 2, lax.rem(learn, 2)
    c, z, y_lo = lax.rem(act, 2), lax.rem(act // 2, 8), act // 16
    y = y_hi * 2 + y_lo
    zh, zl = z // 4, lax.rem(z, 4)
    sibling = device(x, y, z, 1 - c)
    learners = [(lax.rem(learn + d, 8), act) for d in range(1, 8)]
    along_z = [device(x, y, z + d, c) for d in range(1, 8)]
    along_x = [device(x + d, y, z, c) for d in range(1, 4)]
    x_up, x_down = device(x + 1, y, z, c), device(x - 1, y, z, c)
    along_y = [device(x, y + d, z, c) for d in range(1, 4)]
    y_up, y_down = along_y[0], along_y[2]
    xu, xd = lax.rem(x + 1, 4), lax.rem(x + 3, 4)
    yu, yd = lax.rem(y + 1, 4), lax.rem(y + 3, 4)
    x_rows, y_rows = pl.ds(0, SPLIT), pl.ds(SPLIT, 72 - SPLIT)

    barrier = pltpu.get_barrier_semaphore()
    peers = learners + along_z + [y_up, y_down, sibling]
    for peer in peers:
        pl.semaphore_signal(barrier, inc=1, device_id=peer, device_id_type=MESH)

    take = pltpu.make_async_copy(grad_ref.at[learn], own, l_sem)
    take.start()
    pl.semaphore_wait(barrier, len(peers))

    def send(src, dst, s, r, to):
        copy = pltpu.make_async_remote_copy(src_ref=src, dst_ref=dst, send_sem=s, recv_sem=r, device_id=to, device_id_type=MESH)
        copy.start()

    def arrived(ref, sem):
        pltpu.make_async_copy(ref, ref, sem).wait()

    def give(h):
        for d in range(1, 8):
            send(grad_ref.at[lax.rem(learn + d, 8), h], slots.at[h, d - 1], s_grad, r_grad.at[h], learners[d - 1])

    give(0)

    col = lax.broadcasted_iota(jnp.int32, (ROWS, 1), 0)
    valid = lax.rem(col, 20) != 19

    def put(a):
        a = jnp.where(valid, jnp.maximum(a, 0.0), 0.0)
        big[W2:W2 + ROWS, 256:512] = a.astype(jnp.bfloat16)
        big[W2:W2 + ROWS, 0:256] = pltpu.roll(a, 1, 0).astype(jnp.bfloat16)
        big[W2:W2 + ROWS, 512:768] = pltpu.roll(a, ROWS - 1, 0).astype(jnp.bfloat16)

    def conv(layer, which):
        for b in range(16):
            halves = [w[layer, which, b // 8, (b // 4) % 2, b % 4, i].astype(jnp.float32) for i in range(2)]
            packed[144 * b:144 * b + 144, :] = jnp.concatenate(halves, axis=0).astype(jnp.bfloat16)
        acc = jnp.dot(big[0:ROWS, :], packed[0:768, :], preferred_element_type=jnp.float32)
        acc += jnp.dot(big[W2:W2 + ROWS, :], packed[768:1536, :], preferred_element_type=jnp.float32)
        acc += jnp.dot(big[2 * W2:2 * W2 + ROWS, :], packed[1536:2304, :], preferred_element_type=jnp.float32)
        return acc

    big[0:W2, :] = jnp.zeros((W2, 768), jnp.bfloat16)
    big[W2 + ROWS:, :] = jnp.zeros((W2, 768), jnp.bfloat16)
    stem_pad[...] = jnp.zeros_like(stem_pad)
    stem_pad[0:36, :] = stem_ref[...]
    point = lax.broadcasted_iota(jnp.int32, (PADR, 384), 1)
    line = lax.broadcasted_iota(jnp.int32, (PADR, 1), 0) - W2
    spare = lax.rem(line + W2, 20)
    at = jnp.where((line >= 0) & (line < ROWS) & (spare != 19), ((line + W2) // 40 - 1) * 19 + spare, -1)
    spots[...] = jnp.where(point == at, 1.0, 0.0).astype(jnp.bfloat16)
    board = lax.broadcasted_iota(jnp.int32, (8, 384), 0)
    stones = jnp.zeros((8, 384), jnp.float32)
    for q in range(2):
        got = pos_ref[q]
        side = side_ref[q]
        code = jnp.where(got == 1 + side, 1.0, jnp.where(got == 2 - side, 2.0, 3.0))
        code = jnp.concatenate([code, jnp.zeros((1, 384 - 361), jnp.float32)], axis=1)
        stones = jnp.where(board == q, code, stones)
    both = lax.dot_general(spots[...], stones.astype(jnp.bfloat16), (((1,), (1,)), ((), ())), preferred_element_type=jnp.float32)
    which = lax.rem((lax.broadcasted_iota(jnp.int32, (PADR, 1), 0)) // 20, 2)
    code_rows = jnp.where(which == 0, both[:, 0:1], both[:, 1:2])
    code_wide = jnp.broadcast_to(code_rows, (PADR, 128))
    lane = lax.broadcasted_iota(jnp.int32, (ROWS, 128), 1)
    seen = jnp.zeros((ROWS, 128), jnp.float32)
    for b in range(3):
        turned = code_wide if b == 1 else pltpu.roll(code_wide, 1 if b == 0 else PADR - 1, 0)
        for a in range(3):
            seen = jnp.where(lane // 4 == 3 * a + b, turned[W2 * a:W2 * a + ROWS, :], seen)
    plane = lane % 4
    feat = jnp.where(plane == 3, jnp.where(seen > 0.0, 1.0, 0.0), jnp.where(seen == (plane + 1).astype(jnp.float32), 1.0, 0.0)).astype(jnp.bfloat16)
    first = jnp.dot(feat, stem_pad[...], preferred_element_type=jnp.float32)
    stream[...] = first
    put(first)

    def owner_step(h):
        arrived(slots.at[h], r_grad.at[h])
        total = own[h]
        for d in range(7):
            total = total + slots[h, d]
        fresh = master_ref[h] - total / 8
        updated_ref[h] = fresh
        staged[x, h] = fresh.astype(jnp.bfloat16)
        for to in along_x:
            send(staged.at[x, h], staged.at[x, h], s_own, r_own.at[h], to)

    def place(h):
        arrived(staged.at[pl.ds(0, 3), h], r_own.at[h])
        for p in range(4):
            w[2 * p + y_hi, h, y_lo, zh, zl, c, y_rows, :] = staged[p, h, SPLIT:, :]

        @pl.when(zl == x)
        def _():
            for p in range(4):
                w[2 * p + y_hi, h, y_lo, zh, zl, c, x_rows, :] = staged[p, h, 0:SPLIT, :]

    def send_z(k):
        layer, h = (k // 2) * 2 + y_hi, lax.rem(k, 2)
        part = w.at[layer, h, y_lo, zh, zl, c, y_rows]
        whole = w.at[layer, h, y_lo, zh, zl, c, x_rows]

        @pl.when(zl == x)
        def _():
            for to in along_z:
                send(whole, whole, s_sem.at[1], r_sem.at[1, k], to)
        for to in along_z:
            send(part, part, s_sem.at[0], r_sem.at[0, k], to)

    def wait_z(k):
        arrived(w.at[pl.ds(0, 7), 0, 0, 0, 0, c, y_rows], r_sem.at[0, k])

        @pl.when(zl == x)
        def _():
            arrived(w.at[pl.ds(0, 1), 0, 0, 0, 0, c, x_rows], r_sem.at[1, k])

        @pl.when(zl != x)
        def _():
            arrived(w.at[pl.ds(0, 2), 0, 0, 0, 0, c, x_rows], r_sem.at[1, k])

    def send_y1(k):
        layer, h = (k // 2) * 2 + y_hi, lax.rem(k, 2)
        part = w.at[layer, h, y_lo, :, :, c, y_rows]
        whole = w.at[layer, h, y_lo, :, x, c, x_rows]
        for to in along_y:
            send(whole, whole, s_sem.at[3], r_sem.at[3, k], to)
        for to in (y_up, y_down):
            send(part, part, s_sem.at[2], r_sem.at[2, k], to)

    def wait_y1_x(k):
        arrived(w.at[pl.ds(0, 3), 0, 0, :, 0, c, x_rows], r_sem.at[3, k])

    def wait_y1_y(k):
        arrived(w.at[pl.ds(0, 2), 0, 0, :, :, c, y_rows], r_sem.at[2, k])

    def send_y2(k):
        for side, half, to in ((yd, 0, y_up), (yu, 1, y_down)):
            layer, h, lo = (k // 2) * 2 + side // 2, lax.rem(k, 2), lax.rem(side, 2)
            part = w.at[layer, h, lo, half, :, c, y_rows]
            send(part, part, s_sem.at[4], r_sem.at[4, k], to)

    def wait_y2(k):
        arrived(w.at[pl.ds(0, 2), 0, 0, 0, :, c, y_rows], r_sem.at[4, k])

    def send_x1(k):
        layer, h = (k // 2) * 2, lax.rem(k, 2)
        part = w.at[pl.ds(layer, 2), h, :, :, x, c, x_rows]
        for to in (x_up, x_down):
            send(part, part, s_sem.at[6], r_sem.at[6, k], to)

    def wait_x1(k):
        arrived(w.at[pl.ds(0, 4), 0, :, :, 0, c, x_rows], r_sem.at[6, k])

    def send_x2(k):
        layer, h = (k // 2) * 2, lax.rem(k, 2)
        for side, half, to in ((xd, 0, x_up), (xu, 1, x_down)):
            part = w.at[layer + half, h, :, :, side, c, x_rows]
            send(part, part, s_sem.at[7], r_sem.at[7, k], to)

    def wait_x2(k):
        arrived(w.at[pl.ds(0, 2), 0, :, :, 0, c, x_rows], r_sem.at[7, k])

    def send_s(k):
        layer, h = (k // 2) * 2, lax.rem(k, 2)
        part = w.at[pl.ds(layer, 2), h, :, :, :, c]
        send(part, part, s_sem.at[8], r_sem.at[8, k], sibling)

    def wait_s(k):
        arrived(w.at[pl.ds(0, 2), 0, :, :, :, c], r_sem.at[8, k])

    def second(layer):
        out = stream[...] + conv(layer, 1)
        stream[...] = out
        put(out)

    def turn(t, carry):
        k = t - LAG

        @pl.when(t < CHUNKS)
        def _():
            wait_z(t)
            send_y1(t)

        @pl.when((t >= 1) & (t - 1 < CHUNKS))
        def _():
            wait_y1_x(t - 1)
            send_x1(t - 1)
            wait_y1_y(t - 1)
            send_y2(t - 1)

        @pl.when((t >= 2) & (t - 2 < CHUNKS))
        def _():
            wait_x1(t - 2)
            send_x2(t - 2)

        @pl.when(k >= 0)
        def _():
            wait_y2(k)
            wait_x2(k)
            send_s(k)

        @pl.when(t + 2 < CHUNKS)
        def _():
            send_z(t + 2)

        @pl.when((k >= 2) & (lax.rem(k, 2) == 0))
        def _():
            put(conv(k - 1, 0))
            second(k - 1)
            wait_s(k)

        @pl.when(k == 0)
        def _():
            wait_s(k)

        @pl.when((k >= 0) & (lax.rem(k, 2) == 1))
        def _():
            put(conv(k - 1, 0))
            wait_s(k)
            second(k - 1)
        return carry

    take.wait()
    owner_step(0)
    give(1)
    place(0)
    send_z(0)
    owner_step(1)
    wait_z(0)
    send_y1(0)
    send_z(2)
    place(1)
    send_z(1)
    lax.fori_loop(1, CHUNKS + LAG, turn, 0)
    put(conv(7, 0))
    stream[...] = stream[...] + conv(7, 1)

    trunk = jnp.maximum(stream[...], 0.0)
    raw = lax.dot_general(jnp.broadcast_to(pol_ref[...].reshape(1, 256), (8, 256)), trunk, (((1,), (1,)), ((), ())),
                          precision=lax.Precision.HIGHEST, preferred_element_type=jnp.float32)
    spot = lax.broadcasted_iota(jnp.int32, (8, ROWS), 1)
    row = lax.broadcasted_iota(jnp.int32, (8, ROWS), 0)
    raw = jnp.where(lax.rem(spot // 20, 2) == row // 4, raw, 0.0)
    top = raw.astype(jnp.bfloat16).astype(jnp.float32)
    middle = (raw - top).astype(jnp.bfloat16).astype(jnp.float32)
    piece = lax.rem(row, 4)
    parts = jnp.where(piece == 0, top, jnp.where(piece == 1, middle, jnp.where(piece == 2, raw - top - middle, 0.0)))
    points = jnp.dot(parts.astype(jnp.bfloat16), spots[W2:W2 + ROWS, :], preferred_element_type=jnp.float32)
    mine_col = lax.rem(col // 20, 2)
    for q in range(2):
        logits = points[4 * q:4 * q + 1] + points[4 * q + 1:4 * q + 2] + points[4 * q + 2:4 * q + 3]
        logits = 10.0 * jnp.tanh(logits[:, 0:361] / 10.0)
        legal = legal_ref[q] > 0
        pooled = jnp.sum(jnp.where(valid & (mine_col == q), trunk, 0.0), axis=0, keepdims=True) / 361.0
        pass_raw = jnp.sum(pooled * pas_ref[...].reshape(1, 256), axis=1, keepdims=True)
        value_raw = jnp.sum(pooled * val_ref[...].reshape(1, 256), axis=1, keepdims=True)
        pass_logit = 10.0 * jnp.tanh(pass_raw / 10.0)
        total = jnp.sum(jnp.where(legal, jnp.exp(logits), 0.0), axis=1, keepdims=True) + jnp.exp(pass_logit)
        logden = jnp.log(total)
        logp_ref[q, :, 0:361] = jnp.where(legal, logits - logden, 0.0)
        logp_ref[q, :, 361:362] = pass_logit - logden
        value_ref[q:q + 1, :] = jnp.tanh(value_raw)

    arrived(slots, s_grad)
    arrived(staged.at[pl.ds(0, 3)], s_own)
    arrived(w.at[pl.ds(0, 7), :, 0, 0, :, c, y_rows], s_sem.at[0])

    @pl.when(zl == x)
    def _():
        arrived(w.at[pl.ds(0, 7), :, 0, 0, :, c, x_rows], s_sem.at[1])
    arrived(w.at[:, 0, :, :, :, c, y_rows], s_sem.at[2])
    arrived(w.at[:, 0, 0, :, pl.ds(0, 3), c, x_rows], s_sem.at[3])
    arrived(w.at[:, 0, 0, :, :, c, y_rows], s_sem.at[4])
    arrived(w.at[:, 0, :, :, :, c, x_rows], s_sem.at[6])
    arrived(w.at[:, 0, :, :, pl.ds(0, 2), c, x_rows], s_sem.at[7])
    arrived(w.at[:, :, :, :, :, c], s_sem.at[8])


def per_device(positions, to_move, legal_moves, master, gradients, stem, pol, pas, val):
    vmem = pl.BlockSpec(memory_space=pltpu.VMEM)
    f32, bf16, dma = jnp.float32, jnp.bfloat16, pltpu.SemaphoreType.DMA
    updated, logp, value = pl.pallas_call(
        body,
        out_shape=(jax.ShapeDtypeStruct((2, 72, 256), f32), jax.ShapeDtypeStruct((2, 1, 362), f32), jax.ShapeDtypeStruct((2, 1), f32)),
        in_specs=[vmem] * 4 + [pl.BlockSpec(memory_space=pl.ANY)] + [vmem] * 4,
        out_specs=(vmem, vmem, vmem),
        scratch_shapes=[
            pltpu.VMEM((8, 2, 2, 2, 4, 2, 72, 256), bf16),
            pltpu.VMEM((2, 7, 72, 256), f32),
            pltpu.VMEM((4, 2, 72, 256), bf16),
            pltpu.VMEM((2, 72, 256), f32),
            pltpu.VMEM((2304, 256), bf16),
            pltpu.VMEM((PADR, 768), bf16),
            pltpu.VMEM((ROWS, 256), f32),
            pltpu.VMEM((128, 256), bf16),
            pltpu.VMEM((PADR, 384), bf16),
            dma, dma((2,)), dma, dma((2,)), dma, dma((9,)), dma((9, CHUNKS)),
        ],
        compiler_params=pltpu.CompilerParams(collective_id=0, has_side_effects=True, vmem_limit_bytes=56 << 20),
    )(positions, to_move.reshape(2, 1, 1), legal_moves, master.reshape(2, 72, 256), gradients.reshape(8, 2, 72, 256), stem, pol, pas, val)
    return updated.reshape(1, 2, 72, 256), logp, value


def solution(mesh):
    spread = P(None, ("learn", "act"), None)
    in_specs = (spread, P(None, ("learn", "act")), spread, P("learn", None, "act", None),
                P("learn", None, None, "act", None), P(), P(), P(), P())
    out_specs = (P("learn", None, "act", None), spread, P(None, ("learn", "act")))
    return jax.shard_map(per_device, mesh=mesh, in_specs=in_specs, out_specs=out_specs, check_vma=False)
```

```python
import jax
import jax.numpy as jnp
from jax import lax
from jax.experimental import pallas as pl
from jax.experimental.pallas import tpu as pltpu
from jax.sharding import PartitionSpec as P

MESH = pl.DeviceIdType.MESH
ROWS = 760
PADR = 840
W2 = 40
BLOCK = 192
SPLIT = 40
CHUNKS = 8
LAG = 3


def device(x, y, z, c):
    y = lax.rem(y + 4, 4)
    return (lax.rem(x + 4, 4) * 2 + y // 2, (lax.rem(y, 2) * 8 + lax.rem(z + 8, 8)) * 2 + c)


def body(pos_ref, side_ref, legal_ref, master_ref, grad_ref, stem_ref, pol_ref, pas_ref, val_ref,
         updated_ref, logp_ref, value_ref,
         w, slots, staged, own, packed, big, stream, result, stem_pad, spots, s_grad, r_grad, s_own, r_own, l_sem, s_sem, r_sem):
    learn, act = lax.axis_index("learn"), lax.axis_index("act")
    x, y_hi = learn // 2, lax.rem(learn, 2)
    c, z, y_lo = lax.rem(act, 2), lax.rem(act // 2, 8), act // 16
    y = y_hi * 2 + y_lo
    zh, zl = z // 4, lax.rem(z, 4)
    sibling = device(x, y, z, 1 - c)
    learners = [(lax.rem(learn + d, 8), act) for d in range(1, 8)]
    along_z = [device(x, y, z + d, c) for d in range(1, 8)]
    along_x = [device(x + d, y, z, c) for d in range(1, 4)]
    x_up, x_down = device(x + 1, y, z, c), device(x - 1, y, z, c)
    along_y = [device(x, y + d, z, c) for d in range(1, 4)]
    y_up, y_down = along_y[0], along_y[2]
    xu, xd = lax.rem(x + 1, 4), lax.rem(x + 3, 4)
    yu, yd = lax.rem(y + 1, 4), lax.rem(y + 3, 4)
    x_rows, y_rows = pl.ds(0, SPLIT), pl.ds(SPLIT, 72 - SPLIT)

    barrier = pltpu.get_barrier_semaphore()
    peers = learners + along_z + [y_up, y_down, sibling]
    for peer in peers:
        pl.semaphore_signal(barrier, inc=1, device_id=peer, device_id_type=MESH)

    take = pltpu.make_async_copy(grad_ref.at[learn], own, l_sem)
    take.start()
    pl.semaphore_wait(barrier, len(peers))

    def send(src, dst, s, r, to):
        copy = pltpu.make_async_remote_copy(src_ref=src, dst_ref=dst, send_sem=s, recv_sem=r, device_id=to, device_id_type=MESH)
        copy.start()

    def arrived(ref, sem):
        pltpu.make_async_copy(ref, ref, sem).wait()

    def give(h):
        for d in range(1, 8):
            send(grad_ref.at[lax.rem(learn + d, 8), h], slots.at[h, d - 1], s_grad, r_grad.at[h], learners[d - 1])

    give(0)

    col = lax.broadcasted_iota(jnp.int32, (ROWS, 1), 0)
    valid = lax.rem(col, 20) != 19

    def put(a):
        a = jnp.where(valid, jnp.maximum(a, 0.0), 0.0)
        big[W2:W2 + ROWS, 256:512] = a.astype(jnp.bfloat16)
        big[W2:W2 + ROWS, 0:256] = pltpu.roll(a, 1, 0).astype(jnp.bfloat16)
        big[W2:W2 + ROWS, 512:768] = pltpu.roll(a, ROWS - 1, 0).astype(jnp.bfloat16)

    def conv(layer, which):
        for b in range(16):
            halves = [w[layer, which, b // 8, (b // 4) % 2, b % 4, i].astype(jnp.float32) for i in range(2)]
            packed[144 * b:144 * b + 144, :] = jnp.concatenate(halves, axis=0).astype(jnp.bfloat16)
        for m in range(0, ROWS, BLOCK):
            n = min(BLOCK, ROWS - m)
            left = jnp.concatenate([big[W2 * a + m:W2 * a + m + n, :] for a in range(3)], axis=1)
            result[m:m + n, :] = jnp.dot(left, packed[...], preferred_element_type=jnp.float32)
        return result[...]

    big[0:W2, :] = jnp.zeros((W2, 768), jnp.bfloat16)
    big[W2 + ROWS:, :] = jnp.zeros((W2, 768), jnp.bfloat16)
    stem_pad[...] = jnp.zeros_like(stem_pad)
    stem_pad[0:36, :] = stem_ref[...]
    point = lax.broadcasted_iota(jnp.int32, (PADR, 384), 1)
    line = lax.broadcasted_iota(jnp.int32, (PADR, 1), 0) - W2
    spare = lax.rem(line + W2, 20)
    at = jnp.where((line >= 0) & (line < ROWS) & (spare != 19), ((line + W2) // 40 - 1) * 19 + spare, -1)
    spots[...] = jnp.where(point == at, 1.0, 0.0).astype(jnp.bfloat16)
    board = lax.broadcasted_iota(jnp.int32, (8, 384), 0)
    stones = jnp.zeros((8, 384), jnp.float32)
    for q in range(2):
        got = pos_ref[q]
        side = side_ref[q]
        code = jnp.where(got == 1 + side, 1.0, jnp.where(got == 2 - side, 2.0, 3.0))
        code = jnp.concatenate([code, jnp.zeros((1, 384 - 361), jnp.float32)], axis=1)
        stones = jnp.where(board == q, code, stones)
    both = lax.dot_general(spots[...], stones.astype(jnp.bfloat16), (((1,), (1,)), ((), ())), preferred_element_type=jnp.float32)
    which = lax.rem((lax.broadcasted_iota(jnp.int32, (PADR, 1), 0)) // 20, 2)
    code_rows = jnp.where(which == 0, both[:, 0:1], both[:, 1:2])
    code_wide = jnp.broadcast_to(code_rows, (PADR, 128))
    lane = lax.broadcasted_iota(jnp.int32, (ROWS, 128), 1)
    seen = jnp.zeros((ROWS, 128), jnp.float32)
    for b in range(3):
        turned = code_wide if b == 1 else pltpu.roll(code_wide, 1 if b == 0 else PADR - 1, 0)
        for a in range(3):
            seen = jnp.where(lane // 4 == 3 * a + b, turned[W2 * a:W2 * a + ROWS, :], seen)
    plane = lane % 4
    feat = jnp.where(plane == 3, jnp.where(seen > 0.0, 1.0, 0.0), jnp.where(seen == (plane + 1).astype(jnp.float32), 1.0, 0.0)).astype(jnp.bfloat16)
    first = jnp.dot(feat, stem_pad[...], preferred_element_type=jnp.float32)
    stream[...] = first
    put(first)

    def owner_step(h):
        arrived(slots.at[h], r_grad.at[h])
        total = own[h]
        for d in range(7):
            total = total + slots[h, d]
        fresh = master_ref[h] - total / 8
        updated_ref[h] = fresh
        staged[x, h] = fresh.astype(jnp.bfloat16)
        for to in along_x:
            send(staged.at[x, h], staged.at[x, h], s_own, r_own.at[h], to)

    def place(h):
        arrived(staged.at[pl.ds(0, 3), h], r_own.at[h])
        for p in range(4):
            w[2 * p + y_hi, h, y_lo, zh, zl, c, y_rows, :] = staged[p, h, SPLIT:, :]

        @pl.when(zl == x)
        def _():
            for p in range(4):
                w[2 * p + y_hi, h, y_lo, zh, zl, c, x_rows, :] = staged[p, h, 0:SPLIT, :]

    def chunk(k):
        late = k // 4
        pair = (1 - late) * lax.rem(k, 2) + late * (k // 2)
        return 2 * pair, (1 - late) * (k // 2) + late * lax.rem(k, 2)

    def send_z(k):
        first_layer, h = chunk(k)
        layer = first_layer + y_hi
        part = w.at[layer, h, y_lo, zh, zl, c, y_rows]
        whole = w.at[layer, h, y_lo, zh, zl, c, x_rows]

        @pl.when(zl == x)
        def _():
            for to in along_z:
                send(whole, whole, s_sem.at[1], r_sem.at[1, k], to)
        for to in along_z:
            send(part, part, s_sem.at[0], r_sem.at[0, k], to)

    def wait_z(k):
        arrived(w.at[pl.ds(0, 7), 0, 0, 0, 0, c, y_rows], r_sem.at[0, k])

        @pl.when(zl == x)
        def _():
            arrived(w.at[pl.ds(0, 1), 0, 0, 0, 0, c, x_rows], r_sem.at[1, k])

        @pl.when(zl != x)
        def _():
            arrived(w.at[pl.ds(0, 2), 0, 0, 0, 0, c, x_rows], r_sem.at[1, k])

    def send_y1(k):
        first_layer, h = chunk(k)
        layer = first_layer + y_hi
        part = w.at[layer, h, y_lo, :, :, c, y_rows]
        whole = w.at[layer, h, y_lo, :, x, c, x_rows]
        for to in along_y:
            send(whole, whole, s_sem.at[3], r_sem.at[3, k], to)
        for to in (y_up, y_down):
            send(part, part, s_sem.at[2], r_sem.at[2, k], to)

    def wait_y1_x(k):
        arrived(w.at[pl.ds(0, 3), 0, 0, :, 0, c, x_rows], r_sem.at[3, k])

    def wait_y1_y(k):
        arrived(w.at[pl.ds(0, 2), 0, 0, :, :, c, y_rows], r_sem.at[2, k])

    def send_y2(k):
        first_layer, h = chunk(k)
        for side, half, to in ((yd, 0, y_up), (yu, 1, y_down)):
            part = w.at[first_layer + side // 2, h, lax.rem(side, 2), half, :, c, y_rows]
            send(part, part, s_sem.at[4], r_sem.at[4, k], to)

    def wait_y2(k):
        arrived(w.at[pl.ds(0, 2), 0, 0, 0, :, c, y_rows], r_sem.at[4, k])

    def send_x1(k):
        first_layer, h = chunk(k)
        for turn_no, sem in ((0, 5), (1, 6)):
            for half, to in ((turn_no, x_up), (1 - turn_no, x_down)):
                part = w.at[first_layer + half, h, :, :, x, c, x_rows]
                send(part, part, s_sem.at[sem], r_sem.at[sem, k], to)

    def wait_x1(k, sem):
        arrived(w.at[pl.ds(0, 2), 0, :, :, 0, c, x_rows], r_sem.at[sem, k])

    def send_x2(k):
        first_layer, h = chunk(k)
        for side, half, to in ((xd, 0, x_up), (xu, 1, x_down)):
            part = w.at[first_layer + half, h, :, :, side, c, x_rows]
            send(part, part, s_sem.at[7], r_sem.at[7, k], to)

    def wait_x2(k):
        arrived(w.at[pl.ds(0, 2), 0, :, :, 0, c, x_rows], r_sem.at[7, k])

    def send_s(k):
        first_layer, h = chunk(k)
        part = w.at[pl.ds(first_layer, 2), h, :, :, :, c]
        send(part, part, s_sem.at[8], r_sem.at[8, k], sibling)

    def wait_s(k):
        arrived(w.at[pl.ds(0, 2), 0, :, :, :, c], r_sem.at[8, k])

    def second(layer):
        out = stream[...] + conv(layer, 1)
        stream[...] = out
        put(out)

    def turn(t, carry):
        k = t - LAG

        @pl.when(t < CHUNKS)
        def _():
            wait_z(t)
            send_y1(t)

        @pl.when((t >= 1) & (t - 1 < CHUNKS))
        def _():
            wait_y1_x(t - 1)
            send_x1(t - 1)
            wait_y1_y(t - 1)
            send_y2(t - 1)

        @pl.when((t >= 2) & (t - 2 < CHUNKS))
        def _():
            wait_x1(t - 2, 5)
            send_x2(t - 2)

        @pl.when(k >= 0)
        def _():
            wait_y2(k)
            wait_x1(k, 6)
            wait_x2(k)
            send_s(k)

        @pl.when(t + 2 < CHUNKS)
        def _():
            send_z(t + 2)

        even = lax.rem(k, 2) == 0

        @pl.when((k == 3) | (even & (k >= 4)))
        def _():
            layer = k - 1 - lax.rem(k, 2)
            put(conv(layer, 0))
            second(layer)

        @pl.when((k == 0) | (k == 1) | (even & (k >= 4)))
        def _():
            wait_s(k)

        @pl.when((k == 2) | ((k >= 3) & (lax.rem(k, 2) == 1)))
        def _():
            layer = k - 2 + lax.rem(k, 2)
            put(conv(layer, 0))
            wait_s(k)
            second(layer)
        return carry

    take.wait()
    owner_step(0)
    give(1)
    place(0)
    send_z(0)
    send_z(1)
    wait_z(0)
    send_y1(0)
    owner_step(1)
    wait_z(1)
    send_y1(1)
    wait_y1_x(0)
    send_x1(0)
    wait_y1_y(0)
    send_y2(0)
    place(1)
    send_z(2)
    send_z(3)
    lax.fori_loop(2, CHUNKS + LAG, turn, 0)
    put(conv(7, 0))
    stream[...] = stream[...] + conv(7, 1)

    trunk = jnp.maximum(stream[...], 0.0)
    raw = lax.dot_general(jnp.broadcast_to(pol_ref[...].reshape(1, 256), (8, 256)), trunk, (((1,), (1,)), ((), ())),
                          precision=lax.Precision.HIGHEST, preferred_element_type=jnp.float32)
    spot = lax.broadcasted_iota(jnp.int32, (8, ROWS), 1)
    row = lax.broadcasted_iota(jnp.int32, (8, ROWS), 0)
    raw = jnp.where(lax.rem(spot // 20, 2) == row // 4, raw, 0.0)
    top = raw.astype(jnp.bfloat16).astype(jnp.float32)
    middle = (raw - top).astype(jnp.bfloat16).astype(jnp.float32)
    piece = lax.rem(row, 4)
    parts = jnp.where(piece == 0, top, jnp.where(piece == 1, middle, jnp.where(piece == 2, raw - top - middle, 0.0)))
    points = jnp.dot(parts.astype(jnp.bfloat16), spots[W2:W2 + ROWS, :], preferred_element_type=jnp.float32)
    mine_col = lax.rem(col // 20, 2)
    for q in range(2):
        logits = points[4 * q:4 * q + 1] + points[4 * q + 1:4 * q + 2] + points[4 * q + 2:4 * q + 3]
        logits = 10.0 * jnp.tanh(logits[:, 0:361] / 10.0)
        legal = legal_ref[q] > 0
        pooled = jnp.sum(jnp.where(valid & (mine_col == q), trunk, 0.0), axis=0, keepdims=True) / 361.0
        pass_raw = jnp.sum(pooled * pas_ref[...].reshape(1, 256), axis=1, keepdims=True)
        value_raw = jnp.sum(pooled * val_ref[...].reshape(1, 256), axis=1, keepdims=True)
        pass_logit = 10.0 * jnp.tanh(pass_raw / 10.0)
        total = jnp.sum(jnp.where(legal, jnp.exp(logits), 0.0), axis=1, keepdims=True) + jnp.exp(pass_logit)
        logden = jnp.log(total)
        logp_ref[q, :, 0:361] = jnp.where(legal, logits - logden, 0.0)
        logp_ref[q, :, 361:362] = pass_logit - logden
        value_ref[q:q + 1, :] = jnp.tanh(value_raw)

    arrived(slots, s_grad)
    arrived(staged.at[pl.ds(0, 3)], s_own)
    arrived(w.at[pl.ds(0, 7), :, 0, 0, :, c, y_rows], s_sem.at[0])

    @pl.when(zl == x)
    def _():
        arrived(w.at[pl.ds(0, 7), :, 0, 0, :, c, x_rows], s_sem.at[1])
    arrived(w.at[:, 0, :, :, :, c, y_rows], s_sem.at[2])
    arrived(w.at[:, 0, 0, :, pl.ds(0, 3), c, x_rows], s_sem.at[3])
    arrived(w.at[:, 0, 0, :, :, c, y_rows], s_sem.at[4])
    for i in (5, 6, 7):
        arrived(w.at[:, 0, :, :, pl.ds(0, 2), c, x_rows], s_sem.at[i])
    arrived(w.at[:, :, :, :, :, c], s_sem.at[8])


def per_device(positions, to_move, legal_moves, master, gradients, stem, pol, pas, val):
    vmem = pl.BlockSpec(memory_space=pltpu.VMEM)
    f32, bf16, dma = jnp.float32, jnp.bfloat16, pltpu.SemaphoreType.DMA
    updated, logp, value = pl.pallas_call(
        body,
        out_shape=(jax.ShapeDtypeStruct((2, 72, 256), f32), jax.ShapeDtypeStruct((2, 1, 362), f32), jax.ShapeDtypeStruct((2, 1), f32)),
        in_specs=[vmem] * 4 + [pl.BlockSpec(memory_space=pl.ANY)] + [vmem] * 4,
        out_specs=(vmem, vmem, vmem),
        scratch_shapes=[
            pltpu.VMEM((8, 2, 2, 2, 4, 2, 72, 256), bf16),
            pltpu.VMEM((2, 7, 72, 256), f32),
            pltpu.VMEM((4, 2, 72, 256), bf16),
            pltpu.VMEM((2, 72, 256), f32),
            pltpu.VMEM((2304, 256), bf16),
            pltpu.VMEM((PADR, 768), bf16),
            pltpu.VMEM((ROWS, 256), f32),
            pltpu.VMEM((ROWS, 256), f32),
            pltpu.VMEM((128, 256), bf16),
            pltpu.VMEM((PADR, 384), bf16),
            dma, dma((2,)), dma, dma((2,)), dma, dma((9,)), dma((9, CHUNKS)),
        ],
        compiler_params=pltpu.CompilerParams(collective_id=0, has_side_effects=True, vmem_limit_bytes=56 << 20),
    )(positions, to_move.reshape(2, 1, 1), legal_moves, master.reshape(2, 72, 256), gradients.reshape(8, 2, 72, 256), stem, pol, pas, val)
    return updated.reshape(1, 2, 72, 256), logp, value


def solution(mesh):
    spread = P(None, ("learn", "act"), None)
    in_specs = (spread, P(None, ("learn", "act")), spread, P("learn", None, "act", None),
                P("learn", None, None, "act", None), P(), P(), P(), P())
    out_specs = (P("learn", None, "act", None), spread, P(None, ("learn", "act")))
    return jax.shard_map(per_device, mesh=mesh, in_specs=in_specs, out_specs=out_specs, check_vma=False)
```

```python
import jax
import jax.numpy as jnp
from jax import lax
from jax.experimental import pallas as pl
from jax.experimental.pallas import tpu as pltpu
from jax.sharding import PartitionSpec as P

MESH = pl.DeviceIdType.MESH
ROWS = 760
PADR = 840
W2 = 40
BLOCK = 192
SPLIT = 40
CHUNKS = 8
LAG = 3


def device(x, y, z, c):
    y = lax.rem(y + 4, 4)
    return (lax.rem(x + 4, 4) * 2 + y // 2, (lax.rem(y, 2) * 8 + lax.rem(z + 8, 8)) * 2 + c)


def body(pos_ref, side_ref, legal_ref, master_hbm, grad_ref, stem_ref, pol_ref, pas_ref, val_ref,
         updated_hbm, logp_ref, value_ref,
         w, slots, staged, own, packed, big, stream, result, stem_pad, spots, master_ref, updated_ref, s_grad, r_grad, s_own, r_own, l_sem, m_sem, u_sem, s_sem, r_sem):
    learn, act = lax.axis_index("learn"), lax.axis_index("act")
    x, y_hi = learn // 2, lax.rem(learn, 2)
    c, z, y_lo = lax.rem(act, 2), lax.rem(act // 2, 8), act // 16
    y = y_hi * 2 + y_lo
    zh, zl = z // 4, lax.rem(z, 4)
    sibling = device(x, y, z, 1 - c)
    learners = [(lax.rem(learn + d, 8), act) for d in range(1, 8)]
    along_z = [device(x, y, z + d, c) for d in (4, 3, 5, 2, 6, 1, 7)]
    along_x = [device(x + d, y, z, c) for d in range(1, 4)]
    x_up, x_down = device(x + 1, y, z, c), device(x - 1, y, z, c)
    along_y = [device(x, y + d, z, c) for d in range(1, 4)]
    y_up, y_down = along_y[0], along_y[2]
    xu, xd = lax.rem(x + 1, 4), lax.rem(x + 3, 4)
    yu, yd = lax.rem(y + 1, 4), lax.rem(y + 3, 4)
    x_rows, y_rows = pl.ds(0, SPLIT), pl.ds(SPLIT, 72 - SPLIT)

    barrier = pltpu.get_barrier_semaphore()
    peers = along_z[:3] + learners + along_z[3:] + [y_up, y_down, sibling]
    for peer in peers:
        pl.semaphore_signal(barrier, inc=1, device_id=peer, device_id_type=MESH)

    take = pltpu.make_async_copy(grad_ref.at[learn], own, l_sem)
    take.start()
    take_master = pltpu.make_async_copy(master_hbm, master_ref, m_sem)
    take_master.start()
    pl.semaphore_wait(barrier, len(peers))

    def send(src, dst, s, r, to):
        copy = pltpu.make_async_remote_copy(src_ref=src, dst_ref=dst, send_sem=s, recv_sem=r, device_id=to, device_id_type=MESH)
        copy.start()

    def arrived(ref, sem):
        pltpu.make_async_copy(ref, ref, sem).wait()

    def give(h):
        for d in (3, 5, 4, 1, 7, 2, 6):
            send(grad_ref.at[lax.rem(learn + d, 8), h], slots.at[h, d - 1], s_grad, r_grad.at[h], learners[d - 1])

    give(0)

    col = lax.broadcasted_iota(jnp.int32, (ROWS, 1), 0)
    valid = lax.rem(col, 20) != 19

    def put(a):
        a = jnp.where(valid, jnp.maximum(a, 0.0), 0.0)
        big[W2:W2 + ROWS, 256:512] = a.astype(jnp.bfloat16)
        big[W2:W2 + ROWS, 0:256] = pltpu.roll(a, 1, 0).astype(jnp.bfloat16)
        big[W2:W2 + ROWS, 512:768] = pltpu.roll(a, ROWS - 1, 0).astype(jnp.bfloat16)

    def conv(layer, which):
        for b in range(16):
            halves = [w[layer, which, b // 8, (b // 4) % 2, b % 4, i].astype(jnp.float32) for i in range(2)]
            packed[144 * b:144 * b + 144, :] = jnp.concatenate(halves, axis=0).astype(jnp.bfloat16)
        for m in range(0, ROWS, BLOCK):
            n = min(BLOCK, ROWS - m)
            left = jnp.concatenate([big[W2 * a + m:W2 * a + m + n, :] for a in range(3)], axis=1)
            result[m:m + n, :] = jnp.dot(left, packed[...], preferred_element_type=jnp.float32)
        return result[...]

    big[0:W2, :] = jnp.zeros((W2, 768), jnp.bfloat16)
    big[W2 + ROWS:, :] = jnp.zeros((W2, 768), jnp.bfloat16)
    stem_pad[...] = jnp.zeros_like(stem_pad)
    stem_pad[0:36, :] = stem_ref[...]
    point = lax.broadcasted_iota(jnp.int32, (PADR, 384), 1)
    line = lax.broadcasted_iota(jnp.int32, (PADR, 1), 0) - W2
    spare = lax.rem(line + W2, 20)
    at = jnp.where((line >= 0) & (line < ROWS) & (spare != 19), ((line + W2) // 40 - 1) * 19 + spare, -1)
    spots[...] = jnp.where(point == at, 1.0, 0.0).astype(jnp.bfloat16)
    board = lax.broadcasted_iota(jnp.int32, (8, 384), 0)
    stones = jnp.zeros((8, 384), jnp.float32)
    for q in range(2):
        got = pos_ref[q]
        side = side_ref[q]
        code = jnp.where(got == 1 + side, 1.0, jnp.where(got == 2 - side, 2.0, 3.0))
        code = jnp.concatenate([code, jnp.zeros((1, 384 - 361), jnp.float32)], axis=1)
        stones = jnp.where(board == q, code, stones)
    both = lax.dot_general(spots[...], stones.astype(jnp.bfloat16), (((1,), (1,)), ((), ())), preferred_element_type=jnp.float32)
    which = lax.rem((lax.broadcasted_iota(jnp.int32, (PADR, 1), 0)) // 20, 2)
    code_rows = jnp.where(which == 0, both[:, 0:1], both[:, 1:2])
    code_wide = jnp.broadcast_to(code_rows, (PADR, 128))
    lane = lax.broadcasted_iota(jnp.int32, (ROWS, 128), 1)
    seen = jnp.zeros((ROWS, 128), jnp.float32)
    for b in range(3):
        turned = code_wide if b == 1 else pltpu.roll(code_wide, 1 if b == 0 else PADR - 1, 0)
        for a in range(3):
            seen = jnp.where(lane // 4 == 3 * a + b, turned[W2 * a:W2 * a + ROWS, :], seen)
    plane = lane % 4
    feat = jnp.where(plane == 3, jnp.where(seen > 0.0, 1.0, 0.0), jnp.where(seen == (plane + 1).astype(jnp.float32), 1.0, 0.0)).astype(jnp.bfloat16)
    first = jnp.dot(feat, stem_pad[...], preferred_element_type=jnp.float32)
    stream[...] = first
    put(first)

    def owner_step(h):
        arrived(slots.at[h], r_grad.at[h])
        total = own[h]
        for d in range(7):
            total = total + slots[h, d]
        fresh = master_ref[h] - total / 8
        updated_ref[h] = fresh
        pltpu.make_async_copy(updated_ref.at[h], updated_hbm.at[h], u_sem.at[h]).start()
        staged[x, h] = fresh.astype(jnp.bfloat16)
        for to in along_x:
            send(staged.at[x, h], staged.at[x, h], s_own, r_own.at[h], to)

    def place(h):
        arrived(staged.at[pl.ds(0, 3), h], r_own.at[h])
        for p in range(4):
            w[2 * p + y_hi, h, y_lo, zh, zl, c, y_rows, :] = staged[p, h, SPLIT:, :]

        @pl.when(zl == x)
        def _():
            for p in range(4):
                w[2 * p + y_hi, h, y_lo, zh, zl, c, x_rows, :] = staged[p, h, 0:SPLIT, :]

    def chunk(k):
        late = k // 4
        pair = (1 - late) * lax.rem(k, 2) + late * (k // 2)
        return 2 * pair, (1 - late) * (k // 2) + late * lax.rem(k, 2)

    def send_z(k):
        first_layer, h = chunk(k)
        layer = first_layer + y_hi
        part = w.at[layer, h, y_lo, zh, zl, c, y_rows]
        whole = w.at[layer, h, y_lo, zh, zl, c, x_rows]

        @pl.when(zl == x)
        def _():
            for to in along_z:
                send(whole, whole, s_sem.at[1], r_sem.at[1, k], to)
        for to in along_z:
            send(part, part, s_sem.at[0], r_sem.at[0, k], to)

    def wait_z(k):
        arrived(w.at[pl.ds(0, 7), 0, 0, 0, 0, c, y_rows], r_sem.at[0, k])

        @pl.when(zl == x)
        def _():
            arrived(w.at[pl.ds(0, 1), 0, 0, 0, 0, c, x_rows], r_sem.at[1, k])

        @pl.when(zl != x)
        def _():
            arrived(w.at[pl.ds(0, 2), 0, 0, 0, 0, c, x_rows], r_sem.at[1, k])

    def send_y1(k):
        first_layer, h = chunk(k)
        layer = first_layer + y_hi
        part = w.at[layer, h, y_lo, :, :, c, y_rows]
        whole = w.at[layer, h, y_lo, :, x, c, x_rows]
        for to in along_y:
            send(whole, whole, s_sem.at[3], r_sem.at[3, k], to)
        for to in (y_up, y_down):
            send(part, part, s_sem.at[2], r_sem.at[2, k], to)

    def wait_y1_x(k):
        arrived(w.at[pl.ds(0, 3), 0, 0, :, 0, c, x_rows], r_sem.at[3, k])

    def wait_y1_y(k):
        arrived(w.at[pl.ds(0, 2), 0, 0, :, :, c, y_rows], r_sem.at[2, k])

    def send_y2(k):
        first_layer, h = chunk(k)
        for side, half, to in ((yd, 0, y_up), (yu, 1, y_down)):
            part = w.at[first_layer + side // 2, h, lax.rem(side, 2), half, :, c, y_rows]
            send(part, part, s_sem.at[4], r_sem.at[4, k], to)

    def wait_y2(k):
        arrived(w.at[pl.ds(0, 2), 0, 0, 0, :, c, y_rows], r_sem.at[4, k])

    def send_x1(k):
        first_layer, h = chunk(k)
        for turn_no, sem in ((0, 5), (1, 6)):
            for half, to in ((turn_no, x_up), (1 - turn_no, x_down)):
                part = w.at[first_layer + half, h, :, :, x, c, x_rows]
                send(part, part, s_sem.at[sem], r_sem.at[sem, k], to)

    def wait_x1(k, sem):
        arrived(w.at[pl.ds(0, 2), 0, :, :, 0, c, x_rows], r_sem.at[sem, k])

    def send_x2(k):
        first_layer, h = chunk(k)
        for side, half, to in ((xd, 0, x_up), (xu, 1, x_down)):
            part = w.at[first_layer + half, h, :, :, side, c, x_rows]
            send(part, part, s_sem.at[7], r_sem.at[7, k], to)

    def wait_x2(k):
        arrived(w.at[pl.ds(0, 2), 0, :, :, 0, c, x_rows], r_sem.at[7, k])

    def send_s(k, rows, sem):
        first_layer, h = chunk(k)
        part = w.at[pl.ds(first_layer, 2), h, :, :, :, c, rows]
        send(part, part, s_sem.at[sem], r_sem.at[sem, k], sibling)

    def wait_s(k):
        arrived(w.at[pl.ds(0, 2), 0, :, :, :, c, y_rows], r_sem.at[9, k])
        arrived(w.at[pl.ds(0, 2), 0, :, :, :, c, x_rows], r_sem.at[8, k])

    def second(layer):
        out = stream[...] + conv(layer, 1)
        stream[...] = out
        put(out)

    def turn(t, carry):
        k = t - LAG

        @pl.when(t < CHUNKS)
        def _():
            wait_z(t)
            send_y1(t)

        @pl.when((t >= 1) & (t - 1 < CHUNKS))
        def _():
            wait_y1_x(t - 1)
            send_x1(t - 1)
            wait_y1_y(t - 1)
            send_y2(t - 1)

        @pl.when((t >= 2) & (t - 2 < CHUNKS))
        def _():
            wait_x1(t - 2, 5)
            send_x2(t - 2)

        @pl.when(k >= 0)
        def _():
            wait_y2(k)
            send_s(k, y_rows, 9)
            wait_x1(k, 6)
            wait_x2(k)
            send_s(k, x_rows, 8)

        @pl.when(t + 2 < CHUNKS)
        def _():
            send_z(t + 2)

        even = lax.rem(k, 2) == 0

        @pl.when((k == 3) | (even & (k >= 4)))
        def _():
            layer = k - 1 - lax.rem(k, 2)
            put(conv(layer, 0))
            second(layer)

        @pl.when((k == 0) | (k == 1) | (even & (k >= 4)))
        def _():
            wait_s(k)

        @pl.when((k == 2) | ((k >= 3) & (lax.rem(k, 2) == 1)))
        def _():
            layer = k - 2 + lax.rem(k, 2)
            put(conv(layer, 0))
            wait_s(k)
            second(layer)
        return carry

    take.wait()
    take_master.wait()
    owner_step(0)
    give(1)
    place(0)
    send_z(0)
    send_z(1)
    wait_z(0)
    send_y1(0)
    owner_step(1)
    wait_y1_x(0)
    send_x1(0)
    wait_z(1)
    send_y1(1)
    wait_y1_y(0)
    send_y2(0)
    place(1)
    send_z(2)
    send_z(3)
    lax.fori_loop(2, CHUNKS + LAG, turn, 0)
    put(conv(7, 0))
    stream[...] = stream[...] + conv(7, 1)

    trunk = jnp.maximum(stream[...], 0.0)
    raw = lax.dot_general(jnp.broadcast_to(pol_ref[...].reshape(1, 256), (8, 256)), trunk, (((1,), (1,)), ((), ())),
                          precision=lax.Precision.HIGHEST, preferred_element_type=jnp.float32)
    spot = lax.broadcasted_iota(jnp.int32, (8, ROWS), 1)
    row = lax.broadcasted_iota(jnp.int32, (8, ROWS), 0)
    raw = jnp.where(lax.rem(spot // 20, 2) == row // 4, raw, 0.0)
    top = raw.astype(jnp.bfloat16).astype(jnp.float32)
    middle = (raw - top).astype(jnp.bfloat16).astype(jnp.float32)
    piece = lax.rem(row, 4)
    parts = jnp.where(piece == 0, top, jnp.where(piece == 1, middle, jnp.where(piece == 2, raw - top - middle, 0.0)))
    points = jnp.dot(parts.astype(jnp.bfloat16), spots[W2:W2 + ROWS, :], preferred_element_type=jnp.float32)
    mine_col = lax.rem(col // 20, 2)
    for q in range(2):
        logits = points[4 * q:4 * q + 1] + points[4 * q + 1:4 * q + 2] + points[4 * q + 2:4 * q + 3]
        logits = 10.0 * jnp.tanh(logits[:, 0:361] / 10.0)
        legal = legal_ref[q] > 0
        pooled = jnp.sum(jnp.where(valid & (mine_col == q), trunk, 0.0), axis=0, keepdims=True) / 361.0
        pass_raw = jnp.sum(pooled * pas_ref[...].reshape(1, 256), axis=1, keepdims=True)
        value_raw = jnp.sum(pooled * val_ref[...].reshape(1, 256), axis=1, keepdims=True)
        pass_logit = 10.0 * jnp.tanh(pass_raw / 10.0)
        total = jnp.sum(jnp.where(legal, jnp.exp(logits), 0.0), axis=1, keepdims=True) + jnp.exp(pass_logit)
        logden = jnp.log(total)
        logp_ref[q, :, 0:361] = jnp.where(legal, logits - logden, 0.0)
        logp_ref[q, :, 361:362] = pass_logit - logden
        value_ref[q:q + 1, :] = jnp.tanh(value_raw)

    arrived(slots, s_grad)
    for h in range(2):
        pltpu.make_async_copy(updated_ref.at[h], updated_hbm.at[h], u_sem.at[h]).wait()
    arrived(staged.at[pl.ds(0, 3)], s_own)
    arrived(w.at[pl.ds(0, 7), :, 0, 0, :, c, y_rows], s_sem.at[0])

    @pl.when(zl == x)
    def _():
        arrived(w.at[pl.ds(0, 7), :, 0, 0, :, c, x_rows], s_sem.at[1])
    arrived(w.at[:, 0, :, :, :, c, y_rows], s_sem.at[2])
    arrived(w.at[:, 0, 0, :, pl.ds(0, 3), c, x_rows], s_sem.at[3])
    arrived(w.at[:, 0, 0, :, :, c, y_rows], s_sem.at[4])
    for i in (5, 6, 7):
        arrived(w.at[:, 0, :, :, pl.ds(0, 2), c, x_rows], s_sem.at[i])
    arrived(w.at[:, :, :, :, :, c, x_rows], s_sem.at[8])
    arrived(w.at[:, :, :, :, :, c, y_rows], s_sem.at[9])


def per_device(positions, to_move, legal_moves, master, gradients, stem, pol, pas, val):
    vmem = pl.BlockSpec(memory_space=pltpu.VMEM)
    f32, bf16, dma = jnp.float32, jnp.bfloat16, pltpu.SemaphoreType.DMA
    updated, logp, value = pl.pallas_call(
        body,
        out_shape=(jax.ShapeDtypeStruct((2, 72, 256), f32), jax.ShapeDtypeStruct((2, 1, 362), f32), jax.ShapeDtypeStruct((2, 1), f32)),
        in_specs=[vmem] * 3 + [pl.BlockSpec(memory_space=pl.ANY)] * 2 + [vmem] * 4,
        out_specs=(pl.BlockSpec(memory_space=pl.ANY), vmem, vmem),
        scratch_shapes=[
            pltpu.VMEM((8, 2, 2, 2, 4, 2, 72, 256), bf16),
            pltpu.VMEM((2, 7, 72, 256), f32),
            pltpu.VMEM((4, 2, 72, 256), bf16),
            pltpu.VMEM((2, 72, 256), f32),
            pltpu.VMEM((2304, 256), bf16),
            pltpu.VMEM((PADR, 768), bf16),
            pltpu.VMEM((ROWS, 256), f32),
            pltpu.VMEM((ROWS, 256), f32),
            pltpu.VMEM((128, 256), bf16),
            pltpu.VMEM((PADR, 384), bf16),
            pltpu.VMEM((2, 72, 256), f32),
            pltpu.VMEM((2, 72, 256), f32),
            dma, dma((2,)), dma, dma((2,)), dma, dma, dma((2,)), dma((10,)), dma((10, CHUNKS)),
        ],
        compiler_params=pltpu.CompilerParams(collective_id=0, has_side_effects=True, vmem_limit_bytes=56 << 20),
    )(positions, to_move.reshape(2, 1, 1), legal_moves, master.reshape(2, 72, 256), gradients.reshape(8, 2, 72, 256), stem, pol, pas, val)
    return updated.reshape(1, 2, 72, 256), logp, value


def solution(mesh):
    spread = P(None, ("learn", "act"), None)
    in_specs = (spread, P(None, ("learn", "act")), spread, P("learn", None, "act", None),
                P("learn", None, None, "act", None), P(), P(), P(), P())
    out_specs = (P("learn", None, "act", None), spread, P(None, ("learn", "act")))
    return jax.shard_map(per_device, mesh=mesh, in_specs=in_specs, out_specs=out_specs, check_vma=False)
```

```python
import jax
import jax.numpy as jnp
from jax import lax
from jax.experimental import pallas as pl
from jax.experimental.pallas import tpu as pltpu
from jax.sharding import PartitionSpec as P

MESH = pl.DeviceIdType.MESH
ROWS = 760
PADR = 840
W2 = 40
BLOCK = 192
SPLIT = 40
CHUNKS = 8
LAG = 3


def device(x, y, z, c):
    y = lax.rem(y + 4, 4)
    return (lax.rem(x + 4, 4) * 2 + y // 2, (lax.rem(y, 2) * 8 + lax.rem(z + 8, 8)) * 2 + c)


def body(pos_ref, side_ref, legal_ref, master_hbm, grad_ref, stem_ref, pol_ref, pas_ref, val_ref,
         updated_hbm, logp_ref, value_ref,
         w, slots, staged, own, packed, big, stream, result, stem_pad, spots, master_ref, updated_ref, s_grad, r_grad, s_own, r_own, l_sem, m_sem, u_sem, s_sem, r_sem):
    learn, act = lax.axis_index("learn"), lax.axis_index("act")
    x, y_hi = learn // 2, lax.rem(learn, 2)
    c, z, y_lo = lax.rem(act, 2), lax.rem(act // 2, 8), act // 16
    y = y_hi * 2 + y_lo
    zh, zl = z // 4, lax.rem(z, 4)
    sibling = device(x, y, z, 1 - c)
    learners = [(lax.rem(learn + d, 8), act) for d in range(1, 8)]
    along_z = [device(x, y, z + d, c) for d in (4, 3, 5, 2, 6, 1, 7)]
    along_x = [device(x + d, y, z, c) for d in range(1, 4)]
    x_up, x_down = device(x + 1, y, z, c), device(x - 1, y, z, c)
    along_y = [device(x, y + d, z, c) for d in range(1, 4)]
    y_up, y_down = along_y[0], along_y[2]
    xu, xd = lax.rem(x + 1, 4), lax.rem(x + 3, 4)
    yu, yd = lax.rem(y + 1, 4), lax.rem(y + 3, 4)
    x_rows, y_rows = pl.ds(0, SPLIT), pl.ds(SPLIT, 72 - SPLIT)

    barrier = pltpu.get_barrier_semaphore()
    peers = along_z[:3] + learners + along_z[3:] + [y_up, y_down, sibling]
    for peer in peers:
        pl.semaphore_signal(barrier, inc=1, device_id=peer, device_id_type=MESH)

    take = pltpu.make_async_copy(grad_ref.at[learn], own, l_sem)
    take.start()
    take_master = pltpu.make_async_copy(master_hbm, master_ref, m_sem)
    take_master.start()
    pl.semaphore_wait(barrier, len(peers))

    def send(src, dst, s, r, to):
        copy = pltpu.make_async_remote_copy(src_ref=src, dst_ref=dst, send_sem=s, recv_sem=r, device_id=to, device_id_type=MESH)
        copy.start()

    def arrived(ref, sem):
        pltpu.make_async_copy(ref, ref, sem).wait()

    def give(h):
        for d in (3, 5, 4, 1, 7, 2, 6):
            send(grad_ref.at[lax.rem(learn + d, 8), h], slots.at[h, d - 1], s_grad, r_grad.at[h], learners[d - 1])

    give(0)

    col = lax.broadcasted_iota(jnp.int32, (ROWS, 1), 0)
    valid = lax.rem(col, 20) != 19

    def put(a):
        a = jnp.where(valid, jnp.maximum(a, 0.0), 0.0)
        big[W2:W2 + ROWS, 256:512] = a.astype(jnp.bfloat16)
        big[W2:W2 + ROWS, 0:256] = pltpu.roll(a, 1, 0).astype(jnp.bfloat16)
        big[W2:W2 + ROWS, 512:768] = pltpu.roll(a, ROWS - 1, 0).astype(jnp.bfloat16)

    def conv(layer, which):
        for b in range(16):
            halves = [w[layer, which, b // 8, (b // 4) % 2, b % 4, i].astype(jnp.float32) for i in range(2)]
            packed[144 * b:144 * b + 144, :] = jnp.concatenate(halves, axis=0).astype(jnp.bfloat16)
        for m in range(0, ROWS, BLOCK):
            n = min(BLOCK, ROWS - m)
            left = jnp.concatenate([big[W2 * a + m:W2 * a + m + n, :] for a in range(3)], axis=1)
            result[m:m + n, :] = jnp.dot(left, packed[...], preferred_element_type=jnp.float32)
        return result[...]

    big[0:W2, :] = jnp.zeros((W2, 768), jnp.bfloat16)
    big[W2 + ROWS:, :] = jnp.zeros((W2, 768), jnp.bfloat16)
    stem_pad[...] = jnp.zeros_like(stem_pad)
    stem_pad[0:36, :] = stem_ref[...]
    point = lax.broadcasted_iota(jnp.int32, (PADR, 384), 1)
    line = lax.broadcasted_iota(jnp.int32, (PADR, 1), 0) - W2
    spare = lax.rem(line + W2, 20)
    at = jnp.where((line >= 0) & (line < ROWS) & (spare != 19), ((line + W2) // 40 - 1) * 19 + spare, -1)
    spots[...] = jnp.where(point == at, 1.0, 0.0).astype(jnp.bfloat16)
    board = lax.broadcasted_iota(jnp.int32, (8, 384), 0)
    stones = jnp.zeros((8, 384), jnp.float32)
    for q in range(2):
        got = pos_ref[q]
        side = side_ref[q]
        code = jnp.where(got == 1 + side, 1.0, jnp.where(got == 2 - side, 2.0, 3.0))
        code = jnp.concatenate([code, jnp.zeros((1, 384 - 361), jnp.float32)], axis=1)
        stones = jnp.where(board == q, code, stones)
    both = lax.dot_general(spots[...], stones.astype(jnp.bfloat16), (((1,), (1,)), ((), ())), preferred_element_type=jnp.float32)
    which = lax.rem((lax.broadcasted_iota(jnp.int32, (PADR, 1), 0)) // 20, 2)
    code_rows = jnp.where(which == 0, both[:, 0:1], both[:, 1:2])
    code_wide = jnp.broadcast_to(code_rows, (PADR, 128))
    lane = lax.broadcasted_iota(jnp.int32, (ROWS, 128), 1)
    seen = jnp.zeros((ROWS, 128), jnp.float32)
    for b in range(3):
        turned = code_wide if b == 1 else pltpu.roll(code_wide, 1 if b == 0 else PADR - 1, 0)
        for a in range(3):
            seen = jnp.where(lane // 4 == 3 * a + b, turned[W2 * a:W2 * a + ROWS, :], seen)
    plane = lane % 4
    feat = jnp.where(plane == 3, jnp.where(seen > 0.0, 1.0, 0.0), jnp.where(seen == (plane + 1).astype(jnp.float32), 1.0, 0.0)).astype(jnp.bfloat16)
    first = jnp.dot(feat, stem_pad[...], preferred_element_type=jnp.float32)
    stream[...] = first
    put(first)

    def owner_step(h):
        arrived(slots.at[h], r_grad.at[h])
        total = own[h]
        for d in range(7):
            total = total + slots[h, d]
        fresh = master_ref[h] - total / 8
        updated_ref[h] = fresh
        pltpu.make_async_copy(updated_ref.at[h], updated_hbm.at[h], u_sem.at[h]).start()
        staged[x, h] = fresh.astype(jnp.bfloat16)
        for to in along_x:
            send(staged.at[x, h], staged.at[x, h], s_own, r_own.at[h], to)

    def place(h):
        arrived(staged.at[pl.ds(0, 3), h], r_own.at[h])
        for p in range(4):
            w[2 * p + y_hi, h, y_lo, zh, zl, c, y_rows, :] = staged[p, h, SPLIT:, :]

        @pl.when(zl == x)
        def _():
            for p in range(4):
                w[2 * p + y_hi, h, y_lo, zh, zl, c, x_rows, :] = staged[p, h, 0:SPLIT, :]

    def chunk(k):
        late = k // 4
        pair = (1 - late) * lax.rem(k, 2) + late * (k // 2)
        return 2 * pair, (1 - late) * (k // 2) + late * lax.rem(k, 2)

    def send_z(k):
        first_layer, h = chunk(k)
        layer = first_layer + y_hi
        part = w.at[layer, h, y_lo, zh, zl, c, y_rows]
        whole = w.at[layer, h, y_lo, zh, zl, c, x_rows]

        @pl.when(zl == x)
        def _():
            for to in along_z:
                send(whole, whole, s_sem.at[1], r_sem.at[1, k], to)
        for to in along_z:
            send(part, part, s_sem.at[0], r_sem.at[0, k], to)

    def wait_z(k):
        arrived(w.at[pl.ds(0, 7), 0, 0, 0, 0, c, y_rows], r_sem.at[0, k])

        @pl.when(zl == x)
        def _():
            arrived(w.at[pl.ds(0, 1), 0, 0, 0, 0, c, x_rows], r_sem.at[1, k])

        @pl.when(zl != x)
        def _():
            arrived(w.at[pl.ds(0, 2), 0, 0, 0, 0, c, x_rows], r_sem.at[1, k])

    def send_y1(k):
        first_layer, h = chunk(k)
        layer = first_layer + y_hi
        part = w.at[layer, h, y_lo, :, :, c, y_rows]
        whole = w.at[layer, h, y_lo, :, x, c, x_rows]
        for to in (along_y[1], y_up, y_down):
            send(whole, whole, s_sem.at[3], r_sem.at[3, k], to)
        for to in (y_up, y_down):
            send(part, part, s_sem.at[2], r_sem.at[2, k], to)

    def wait_y1_x(k):
        arrived(w.at[pl.ds(0, 3), 0, 0, :, 0, c, x_rows], r_sem.at[3, k])

    def wait_y1_y(k):
        arrived(w.at[pl.ds(0, 2), 0, 0, :, :, c, y_rows], r_sem.at[2, k])

    def send_y2(k):
        first_layer, h = chunk(k)
        for side, half, to in ((yd, 0, y_up), (yu, 1, y_down)):
            part = w.at[first_layer + side // 2, h, lax.rem(side, 2), half, :, c, y_rows]
            send(part, part, s_sem.at[4], r_sem.at[4, k], to)

    def wait_y2(k):
        arrived(w.at[pl.ds(0, 2), 0, 0, 0, :, c, y_rows], r_sem.at[4, k])

    def send_x1(k, sem):
        first_layer, h = chunk(k)
        for half, to in ((sem - 5, x_up), (6 - sem, x_down)):
            part = w.at[first_layer + half, h, :, :, x, c, x_rows]
            send(part, part, s_sem.at[sem], r_sem.at[sem, k], to)

    def wait_x1(k, sem):
        arrived(w.at[pl.ds(0, 2), 0, :, :, 0, c, x_rows], r_sem.at[sem, k])

    def send_x2(k):
        first_layer, h = chunk(k)
        for side, half, to in ((xd, 0, x_up), (xu, 1, x_down)):
            part = w.at[first_layer + half, h, :, :, side, c, x_rows]
            send(part, part, s_sem.at[7], r_sem.at[7, k], to)

    def wait_x2(k):
        arrived(w.at[pl.ds(0, 2), 0, :, :, 0, c, x_rows], r_sem.at[7, k])

    def send_s(k, rows, sem):
        first_layer, h = chunk(k)
        part = w.at[pl.ds(first_layer, 2), h, :, :, :, c, rows]
        send(part, part, s_sem.at[sem], r_sem.at[sem, k], sibling)

    def wait_s(k):
        arrived(w.at[pl.ds(0, 2), 0, :, :, :, c, y_rows], r_sem.at[9, k])
        arrived(w.at[pl.ds(0, 2), 0, :, :, :, c, x_rows], r_sem.at[8, k])

    def second(layer):
        out = stream[...] + conv(layer, 1)
        stream[...] = out
        put(out)

    def turn(t, carry):
        k = t - LAG

        @pl.when(t < CHUNKS)
        def _():
            wait_z(t)
            send_y1(t)

        @pl.when((t >= 1) & (t - 1 < CHUNKS))
        def _():
            wait_y1_x(t - 1)
            send_x1(t - 1, 5)

        @pl.when((t >= 2) & (t - 2 < CHUNKS))
        def _():
            wait_x1(t - 2, 5)
            send_x2(t - 2)

        @pl.when((t >= 1) & (t - 1 < CHUNKS))
        def _():
            send_x1(t - 1, 6)
            wait_y1_y(t - 1)
            send_y2(t - 1)

        @pl.when(k >= 0)
        def _():
            wait_y2(k)
            send_s(k, y_rows, 9)
            wait_x1(k, 6)
            wait_x2(k)
            send_s(k, x_rows, 8)

        @pl.when(t + 2 < CHUNKS)
        def _():
            send_z(t + 2)

        even = lax.rem(k, 2) == 0

        @pl.when((k == 3) | (even & (k >= 4)))
        def _():
            layer = k - 1 - lax.rem(k, 2)
            put(conv(layer, 0))
            second(layer)

        @pl.when((k == 0) | (k == 1) | (even & (k >= 4)))
        def _():
            wait_s(k)

        @pl.when((k == 2) | ((k >= 3) & (lax.rem(k, 2) == 1)))
        def _():
            layer = k - 2 + lax.rem(k, 2)
            put(conv(layer, 0))
            wait_s(k)
            second(layer)
        return carry

    take.wait()
    take_master.wait()
    owner_step(0)
    give(1)
    place(0)
    send_z(0)
    send_z(1)
    wait_z(0)
    send_y1(0)
    owner_step(1)
    wait_y1_x(0)
    send_x1(0, 5)
    send_x1(0, 6)
    wait_z(1)
    send_y1(1)
    wait_y1_y(0)
    send_y2(0)
    place(1)
    send_z(2)
    send_z(3)
    lax.fori_loop(2, CHUNKS + LAG, turn, 0)
    put(conv(7, 0))
    stream[...] = stream[...] + conv(7, 1)

    trunk = jnp.maximum(stream[...], 0.0)
    raw = lax.dot_general(jnp.broadcast_to(pol_ref[...].reshape(1, 256), (8, 256)), trunk, (((1,), (1,)), ((), ())),
                          precision=lax.Precision.HIGHEST, preferred_element_type=jnp.float32)
    spot = lax.broadcasted_iota(jnp.int32, (8, ROWS), 1)
    row = lax.broadcasted_iota(jnp.int32, (8, ROWS), 0)
    raw = jnp.where(lax.rem(spot // 20, 2) == row // 4, raw, 0.0)
    top = raw.astype(jnp.bfloat16).astype(jnp.float32)
    middle = (raw - top).astype(jnp.bfloat16).astype(jnp.float32)
    piece = lax.rem(row, 4)
    parts = jnp.where(piece == 0, top, jnp.where(piece == 1, middle, jnp.where(piece == 2, raw - top - middle, 0.0)))
    points = jnp.dot(parts.astype(jnp.bfloat16), spots[W2:W2 + ROWS, :], preferred_element_type=jnp.float32)
    mine_col = lax.rem(col // 20, 2)
    for q in range(2):
        logits = points[4 * q:4 * q + 1] + points[4 * q + 1:4 * q + 2] + points[4 * q + 2:4 * q + 3]
        logits = 10.0 * jnp.tanh(logits[:, 0:361] / 10.0)
        legal = legal_ref[q] > 0
        pooled = jnp.sum(jnp.where(valid & (mine_col == q), trunk, 0.0), axis=0, keepdims=True) / 361.0
        pass_raw = jnp.sum(pooled * pas_ref[...].reshape(1, 256), axis=1, keepdims=True)
        value_raw = jnp.sum(pooled * val_ref[...].reshape(1, 256), axis=1, keepdims=True)
        pass_logit = 10.0 * jnp.tanh(pass_raw / 10.0)
        total = jnp.sum(jnp.where(legal, jnp.exp(logits), 0.0), axis=1, keepdims=True) + jnp.exp(pass_logit)
        logden = jnp.log(total)
        logp_ref[q, :, 0:361] = jnp.where(legal, logits - logden, 0.0)
        logp_ref[q, :, 361:362] = pass_logit - logden
        value_ref[q:q + 1, :] = jnp.tanh(value_raw)

    arrived(slots, s_grad)
    for h in range(2):
        pltpu.make_async_copy(updated_ref.at[h], updated_hbm.at[h], u_sem.at[h]).wait()
    arrived(staged.at[pl.ds(0, 3)], s_own)
    arrived(w.at[pl.ds(0, 7), :, 0, 0, :, c, y_rows], s_sem.at[0])

    @pl.when(zl == x)
    def _():
        arrived(w.at[pl.ds(0, 7), :, 0, 0, :, c, x_rows], s_sem.at[1])
    arrived(w.at[:, 0, :, :, :, c, y_rows], s_sem.at[2])
    arrived(w.at[:, 0, 0, :, pl.ds(0, 3), c, x_rows], s_sem.at[3])
    arrived(w.at[:, 0, 0, :, :, c, y_rows], s_sem.at[4])
    for i in (5, 6, 7):
        arrived(w.at[:, 0, :, :, pl.ds(0, 2), c, x_rows], s_sem.at[i])
    arrived(w.at[:, :, :, :, :, c, x_rows], s_sem.at[8])
    arrived(w.at[:, :, :, :, :, c, y_rows], s_sem.at[9])


def per_device(positions, to_move, legal_moves, master, gradients, stem, pol, pas, val):
    vmem = pl.BlockSpec(memory_space=pltpu.VMEM)
    f32, bf16, dma = jnp.float32, jnp.bfloat16, pltpu.SemaphoreType.DMA
    updated, logp, value = pl.pallas_call(
        body,
        out_shape=(jax.ShapeDtypeStruct((2, 72, 256), f32), jax.ShapeDtypeStruct((2, 1, 362), f32), jax.ShapeDtypeStruct((2, 1), f32)),
        in_specs=[vmem] * 3 + [pl.BlockSpec(memory_space=pl.ANY)] * 2 + [vmem] * 4,
        out_specs=(pl.BlockSpec(memory_space=pl.ANY), vmem, vmem),
        scratch_shapes=[
            pltpu.VMEM((8, 2, 2, 2, 4, 2, 72, 256), bf16),
            pltpu.VMEM((2, 7, 72, 256), f32),
            pltpu.VMEM((4, 2, 72, 256), bf16),
            pltpu.VMEM((2, 72, 256), f32),
            pltpu.VMEM((2304, 256), bf16),
            pltpu.VMEM((PADR, 768), bf16),
            pltpu.VMEM((ROWS, 256), f32),
            pltpu.VMEM((ROWS, 256), f32),
            pltpu.VMEM((128, 256), bf16),
            pltpu.VMEM((PADR, 384), bf16),
            pltpu.VMEM((2, 72, 256), f32),
            pltpu.VMEM((2, 72, 256), f32),
            dma, dma((2,)), dma, dma((2,)), dma, dma, dma((2,)), dma((10,)), dma((10, CHUNKS)),
        ],
        compiler_params=pltpu.CompilerParams(collective_id=0, has_side_effects=True, vmem_limit_bytes=56 << 20),
    )(positions, to_move.reshape(2, 1, 1), legal_moves, master.reshape(2, 72, 256), gradients.reshape(8, 2, 72, 256), stem, pol, pas, val)
    return updated.reshape(1, 2, 72, 256), logp, value


def solution(mesh):
    spread = P(None, ("learn", "act"), None)
    in_specs = (spread, P(None, ("learn", "act")), spread, P("learn", None, "act", None),
                P("learn", None, None, "act", None), P(), P(), P(), P())
    out_specs = (P("learn", None, "act", None), spread, P(None, ("learn", "act")))
    return jax.shard_map(per_device, mesh=mesh, in_specs=in_specs, out_specs=out_specs, check_vma=False)
```
